32 devices in a mesh: row: 4 (over y, core), col: 8 (over z, x).
Axes of the slice: x: 2, y: 2, z: 4, core: 2. Of those that a mesh axis runs over, the one named last changes fastest.
Arguments:
- amplitudes: float32 [256, 2, 16384], P('row', None, 'col'), may hold values from -6 to 6
- integrals: bfloat16 [2, 16384, 16384], P(None, 'col', 'row'), may hold values from -0.046875 to 0.046875
- screen: int32 [2, 128, 128], P(None, 'col', 'row'), may hold values 0 or 1
- mirror: int32 [16384], replicated, may hold values from 0 to 16383, as said below
- denominators: float32 [256, 2, 16384], P('col', None, 'row'), may hold values from 0.5 to 4
Outputs:
- update: float32 [256, 2, 16384], P('col', None, 'row')
The draws below stay inside these ranges and needn't reach their ends.
Inputs may be any that keep to these rules, and one draw needn't show every extreme that they name: mirror is a permutation; mirror[p] lies in the tile of 128 positions numbered (p // 128 + 16384 // 256) modulo 16384 // 128.
All inputs are finite; a program needn't handle non-finite values. No bound on the sum of `screen` on one device may be relied on, other than what follows from the above.
Results may differ from the reference program's by a relative error of at most 0.0029.
Values may be sent and summed in bfloat16 or wider, within the bound.
A program may use at most 192 MiB of HBM per device.

```python
import math
import jax
import jax.numpy as jnp
from jax import lax

OCC_PAIRS = 256
PAIRS = 16384
TILE = 128


def draw_mirror(key, part):
    tile_count = PAIRS // TILE
    tile_keys = jax.random.split(jax.random.fold_in(key, 7), tile_count)
    within = jax.vmap(lambda k: jax.random.permutation(k, TILE))(tile_keys).astype(jnp.int32)
    target = (jnp.arange(tile_count, dtype=jnp.int32) + tile_count // 2) % tile_count
    return (target[:, None] * TILE + within).reshape(PAIRS).astype(jnp.int32)


def plant(drawn, key, least, top_value):
    extent = drawn.shape
    spot = [jax.random.randint(jax.random.fold_in(key, axis), (), 0, extent[axis]) for axis in range(len(extent))]
    drawn = drawn.at[tuple(spot)].set(least)
    longest = extent.index(max(extent))
    spot[longest] = (spot[longest] + 1) % extent[longest]
    return drawn.at[tuple(spot)].set(top_value)


def block_levels(rng, shape, cuts, least, top_value):
    def one(dim, shards_of):
        steps = jax.random.uniform(jax.random.fold_in(jax.random.fold_in(rng, 6), dim), (shards_of,), jnp.float32, least / len(cuts), top_value / len(cuts))
        return jnp.repeat(jnp.exp(steps), shape[dim] // shards_of).reshape((-1,) + (1,) * (len(shape) - dim - 1))

    level = one(*cuts[0])
    for cut in cuts[1:]:
        level = level * one(*cut)
    return level


def gaussian(rng, extent, scale, reach, cuts=(), kind=jnp.bfloat16):
    result = scale * jax.random.normal(rng, extent, jnp.float32)
    if cuts:
        result = result * block_levels(rng, extent, cuts, -0.22, 0.18)
    return jnp.clip(result, -reach, reach).astype(kind)


def setup_inputs(seed: int = 0) -> dict:
    keys = jax.random.split(jax.random.key(seed), 6)
    amplitudes = gaussian(keys[0], (OCC_PAIRS, 2, PAIRS), 1.0, 6.0, ((0, 4), (2, 8)), jnp.float32)
    integrals = gaussian(keys[1], (2, PAIRS, PAIRS), PAIRS ** -0.5, 0.046875, ((1, 8), (2, 4)))
    screen = plant((jax.random.randint(keys[2], (2, PAIRS // TILE, PAIRS // TILE), 0, 3) < 2).astype(jnp.int32), jax.random.fold_in(keys[2], 1), 0, 1)
    mirror = draw_mirror(jax.random.fold_in(keys[5], 71), 0)
    denominators = jnp.clip(jnp.exp(math.log(4.0) - 2.0794415 * jax.random.uniform(keys[4], (OCC_PAIRS, 2, PAIRS), jnp.float32) ** block_levels(keys[4], (OCC_PAIRS, 2, PAIRS), ((0, 8), (2, 4)), -0.2, 0.2)), 0.5, 4.0)
    return dict(amplitudes=amplitudes, integrals=integrals, screen=screen, mirror=mirror, denominators=denominators)


def one_sign(signed_part, block, kept_tiles):
    tile_count = PAIRS // TILE

    def step(total, tile):
        start = (tile * TILE).astype(jnp.int32)
        rows = lax.dynamic_slice_in_dim(block, start, TILE, 0)
        keep = jnp.repeat(lax.dynamic_slice_in_dim(kept_tiles, tile, 1, 0)[0].astype(rows.dtype), TILE)
        columns = lax.dynamic_slice_in_dim(signed_part, start, TILE, 1)
        product = jnp.dot(columns, rows * keep[None, :], preferred_element_type=jnp.float32)
        return total + product, None

    total, _ = lax.scan(step, jnp.zeros((OCC_PAIRS, PAIRS), jnp.float32), jnp.arange(tile_count, dtype=jnp.int32))
    return total


def reference(amplitudes, integrals, screen, mirror, denominators):
    direct = amplitudes[:, 0, :]
    flipped = jnp.take(amplitudes[:, 1, :], mirror, axis=1)
    plus_amp = (direct + flipped).astype(jnp.bfloat16)
    minus_amp = (direct - flipped).astype(jnp.bfloat16)
    plus_sum = one_sign(plus_amp, integrals[0], screen[0])
    minus_sum = one_sign(minus_amp, integrals[1], screen[1])
    first = 0.5 * (plus_sum + minus_sum)
    second = jnp.zeros_like(first).at[:, mirror].set(0.5 * (plus_sum - minus_sum))
    return jnp.stack([first, second], axis=1) / denominators
```

```python
import functools

import jax
import jax.numpy as jnp
from jax import lax
from jax.experimental import pallas as pl
from jax.experimental.pallas import tpu as pltpu
from jax.sharding import PartitionSpec as P

TILE = 128
CHUNK = 512
F32, BF16 = jnp.float32, jnp.bfloat16


def flip(x, bits):
    result = x
    place = 0
    while bits >> place:
        if bits >> place & 1:
            result = result + (1 - 2 * (x // (1 << place) % 2)) * (1 << place)
        place += 1
    return result


def position(owner, me, bits):
    total = 0
    for i in range(bits):
        differs = (owner // (1 << i) + me // (1 << i)) % 2
        total = total + differs * (1 << (bits - 1 - i))
    return total


def kernel(sizes, amps, mirror, screen, integrals, out,
           loaded, held, away_src, away_dst, flip_src, flip_dst, signed, acc, inverse, *rest):
    rows, cols, groups, per_row, part, tiles, ab_tiles, early = sizes
    row_bits, col_bits = rows.bit_length() - 1, cols.bit_length() - 1
    sends, recvs = rest[:col_bits], rest[col_bits:2 * col_bits]
    msend, mrecv, a_sem, k_sem, f_sem, g_sem, r_sem, m_sem = rest[2 * col_bits:]
    cd_width = tiles * TILE
    chunk = held.shape[-1]
    lanes = chunk // TILE
    chunks = ab_tiles // lanes
    pieces = groups * chunks
    row_me, col_me = lax.axis_index("row"), lax.axis_index("col")
    half = cols * part // 2

    def a_copy():
        return pltpu.make_async_copy(amps, loaded, a_sem.at[0])

    def k_copy(c, s):
        return pltpu.make_async_copy(
            integrals.at[s, :, pl.ds(pl.multiple_of(c * chunk, chunk), chunk)], held.at[c, s], k_sem.at[c, s])

    def start_k(c, carry):
        for s in range(2):
            k_copy(c, s).start()
        return carry

    a_copy().start()
    lax.fori_loop(0, chunks, start_k, 0)

    barrier = pltpu.get_barrier_semaphore()
    for b in range(col_bits):
        pl.semaphore_signal(barrier, inc=1, device_id={"col": flip(col_me, 1 << b)}, device_id_type=pl.DeviceIdType.MESH)
    for b in range(row_bits):
        pl.semaphore_signal(barrier, inc=1, device_id={"row": flip(row_me, 1 << b)}, device_id_type=pl.DeviceIdType.MESH)

    def remote(src, dst, sem, target):
        return pltpu.make_async_remote_copy(
            src_ref=src, dst_ref=dst, send_sem=sem[0], recv_sem=sem[1],
            device_id=target, device_id_type=pl.DeviceIdType.MESH)

    flips = [(g, k) for g in range(groups) for k in reversed(range(per_row))]

    def member(k):
        total = 0
        for i in range(per_row.bit_length() - 1):
            total = total + (k // (1 << i) % 2 + col_me // (1 << i)) % 2 * (1 << i)
        return total

    def amp_rows(g, k, t, which):
        first = (member(k) * groups + g) * part
        return loaded[pl.ds(first * (2 * tiles) + 2 * t + which, part, stride=2 * tiles), :]

    def f_copy(n):
        src, dst = (away_src, away_dst) if n == 0 else (flip_src.at[n - 1], flip_dst.at[n - 1])
        return remote(src, dst, (f_sem.at[0, n], f_sem.at[1, n]), {"col": flip(col_me, cols // 2)})

    def stage_flip(n):
        g, k = flips[n]
        for t in range(tiles):
            at = pl.ds(t * TILE, TILE)
            value = amp_rows(g, k, t, 1)
            if n == 0:
                away_src[:, at] = value.astype(BF16)
            else:
                flip_src[n - 1, :, at] = value

    def gather_copies(g, stage, k):
        bit = row_bits - 1 - stage
        copies = []
        for t in range(1 << stage):
            shard = flip(row_me, t << (bit + 1))
            pos = position(shard * per_row + member(k), col_me, col_bits)
            i = (g * rows + (1 << stage) - 1 + t) * per_row + k
            block = signed.at[g, :, pos]
            copies.append(remote(block, block, (g_sem.at[0, i], g_sem.at[1, i]), {"row": flip(row_me, 1 << bit)}))
        return copies

    def gather_start(g, stage, k):
        for copy in gather_copies(g, stage, k):
            copy.start()

    def gather_wait(g, stage, k):
        for copy in gather_copies(g, stage, k):
            copy.wait()

    def make_signed(n):
        g, k = flips[n]
        f_copy(n).wait_recv()
        if n + 1 < len(flips):
            f_copy(n + 1).start()
        pos = position(row_me * per_row + member(k), col_me, col_bits)
        for t in range(tiles):
            at = pl.ds(t * TILE, TILE)
            index = jnp.broadcast_to(mirror[pl.ds(col_me * tiles + t, 1), :] % TILE, (part, TILE))
            arrived = away_dst[:, at].astype(F32) if n == 0 else flip_dst[n - 1, :, at]
            flipped = jnp.take_along_axis(arrived, index, axis=1)
            mine = amp_rows(g, k, t, 0)
            signed[g, 0, pos, :, at] = (mine + flipped).astype(BF16)
            signed[g, 1, pos, :, at] = (mine - flipped).astype(BF16)

    def keep_tiles(c):
        for s in range(2):
            k_copy(c, s).wait()

            def one(t, carry):
                for l in range(lanes):
                    factor = jnp.full((16, TILE), screen[s, t, c * lanes + l]).astype(F32).astype(BF16)
                    at = (c, s, pl.ds(pl.multiple_of(t * TILE, TILE), TILE), pl.ds(l * TILE, TILE))
                    block = held[at].reshape(TILE // 16, 16, TILE)
                    held[at] = (block * factor[None]).reshape(TILE, TILE)
                return carry

            lax.fori_loop(0, tiles, one, 0)

    def keep_range(lo, hi):
        def one(c, carry):
            keep_tiles(c)
            return carry

        if hi > lo:
            lax.fori_loop(lo, hi, one, 0)

    def invert(t, carry):
        index = jnp.broadcast_to(mirror[pl.ds(row_me * ab_tiles + t, 1), :] % TILE, (TILE, TILE))
        hit = jnp.where(lax.broadcasted_iota(jnp.int32, (TILE, TILE), 0) == index, 1.0, 0.0).astype(BF16)
        places = lax.broadcasted_iota(jnp.int32, (16, TILE), 1).astype(F32).astype(BF16)
        found = lax.dot_general(places, hit, (((1,), (1,)), ((), ())), preferred_element_type=F32)
        inverse[pl.ds(t, 1), :] = found[:1].astype(jnp.int32)
        return carry

    def stage_copy(b, q):
        return remote(sends[b].at[q], recvs[b].at[q], (r_sem.at[0, b, q], r_sem.at[1, b, q]),
                      {"col": flip(col_me, 1 << b)})

    def mirror_copy(q):
        return remote(msend.at[q], mrecv.at[q], (m_sem.at[0, q], m_sem.at[1, q]),
                      {"row": flip(row_me, rows // 2)})

    def multiply_away(q, carry):
        for s in range(2):
            lhs = signed[0, s, cols // 2:].reshape(half, cd_width)
            sends[0][q, s] = jnp.dot(lhs, held[q, s], preferred_element_type=F32).astype(BF16)
        stage_copy(0, q).start()
        return carry

    def multiply_own(q, carry):
        for s in range(2):
            lhs = signed[0, s, :cols // 2].reshape(half, cd_width)
            acc[q, s] = jnp.dot(lhs, held[q, s], preferred_element_type=F32)
        return carry

    def multiply(q):
        g, c = q // chunks, q % chunks
        for s in range(2):
            lhs = signed[g, s].reshape(cols * part, cd_width)
            total = jnp.dot(lhs, held[c, s], preferred_element_type=F32)
            sends[0][q, s] = total[half:].astype(BF16)
            acc[q, s] = total[:half]
        stage_copy(0, q).start()

    def reduce(b, q):
        stage_copy(b - 1, q).wait()
        few = (cols >> b) * part // 2
        for s in range(2):
            sends[b][q, s] = (acc[q, s, few:2 * few] + recvs[b - 1][q, s, few:2 * few].astype(F32)).astype(BF16)
        stage_copy(b, q).start()
        for s in range(2):
            acc[q, s, :few] = acc[q, s, :few] + recvs[b - 1][q, s, :few].astype(F32)

    def out_rows(q, l, which):
        g, c = q // chunks, q % chunks
        return pl.ds(g * (part * 2 * ab_tiles) + 2 * (c * lanes + l) + which, part, stride=2 * ab_tiles)

    def combine(q):
        c = q % chunks
        stage_copy(col_bits - 1, q).wait()
        for l in range(lanes):
            at = pl.ds(l * TILE, TILE)
            plus = acc[q, 0, :part, at] + recvs[-1][q, 0, :, at].astype(F32)
            minus = acc[q, 1, :part, at] + recvs[-1][q, 1, :, at].astype(F32)
            index = jnp.broadcast_to(inverse[pl.ds(c * lanes + l, 1), :], (part, TILE))
            msend[q, :, at] = jnp.take_along_axis(0.5 * (plus - minus), index, axis=1)
            out[out_rows(q, l, 0), :] = 0.5 * (plus + minus)
        mirror_copy(q).start()

    def place(q):
        mirror_copy(q).wait()
        for l in range(lanes):
            out[out_rows(q, l, 1), :] = mrecv[q, :, pl.ds(l * TILE, TILE)]

    a_copy().wait()
    stage_flip(0)
    pl.semaphore_wait(barrier, col_bits + row_bits)
    f_copy(0).start()
    for n in range(1, len(flips)):
        stage_flip(n)
    lax.fori_loop(0, ab_tiles, invert, 0)

    cut = lambda x: chunks * x // 8
    keep_range(0, cut(3))
    make_signed(0)
    gather_start(0, 0, per_row - 1)
    keep_range(cut(3), cut(6))
    for stage in range(1, row_bits):
        gather_wait(0, stage - 1, per_row - 1)
        gather_start(0, stage, per_row - 1)
    keep_range(cut(6), chunks)
    gather_wait(0, row_bits - 1, per_row - 1)
    for k in reversed(range(1, per_row - 1)):
        make_signed(per_row - 1 - k)
        for stage in range(row_bits):
            gather_start(0, stage, k)
            gather_wait(0, stage, k)
    if per_row > 1:
        lax.fori_loop(0, early // 2, multiply_away, 0)
        make_signed(per_row - 1)
        gather_start(0, 0, 0)
        lax.fori_loop(early // 2, early, multiply_away, 0)
        for stage in range(1, row_bits):
            gather_wait(0, stage - 1, 0)
            gather_start(0, stage, 0)
        gather_wait(0, row_bits - 1, 0)
        lax.fori_loop(0, early, multiply_own, 0)

    events = []
    for g in range(1, groups):
        last = g * chunks
        first = g * per_row
        for k in reversed(range(per_row)):
            n = first + per_row - 1 - k
            begin = last - 1 - 3 * k if k else last - 1
            events.append((begin, functools.partial(make_signed, n)))
            for stage in range(row_bits):
                if stage:
                    events.append((min(begin + stage, last), functools.partial(gather_wait, g, stage - 1, k)))
                events.append((min(begin + stage, last), functools.partial(gather_start, g, stage, k)))
            events.append((last, functools.partial(gather_wait, g, row_bits - 1, k)))

    def step(i, carry):
        for when in sorted(set(w for w, _ in events)):
            @pl.when(i == when)
            def _():
                for w, action in events:
                    if w == when:
                        action()

        @pl.when((i >= early) & (i < pieces))
        def _():
            multiply(i)

        lag = 0
        for b in range(1, col_bits):
            lag += 2 if b == 1 else 1

            @pl.when((i >= lag) & (i < pieces + lag))
            def _():
                reduce(b, i - lag)

        lag += 1

        @pl.when((i >= lag) & (i < pieces + lag))
        def _():
            combine(i - lag)

        lag += 1

        @pl.when((i >= lag) & (i < pieces + lag))
        def _():
            place(i - lag)

        return carry

    lax.fori_loop(min(early, 2), pieces + col_bits + 2, step, 0)
    for n in range(len(flips)):
        f_copy(n).wait_send()


def body(amplitudes, integrals, screen, mirror, denominators):
    cols, rows = lax.axis_size("col"), lax.axis_size("row")
    col_bits = cols.bit_length() - 1
    occ, _, cd_width = amplitudes.shape
    own, _, ab_width = denominators.shape
    per_row = occ // own
    groups = 2 if own % 32 == 0 else 1
    part = own // groups
    chunk = min(CHUNK, ab_width)
    chunks = ab_width // chunk
    pieces = groups * chunks
    tiles, ab_tiles = cd_width // TILE, ab_width // TILE
    early = min(4, chunks) if per_row > 1 else 0
    flips = groups * per_row
    vmem = pl.BlockSpec(memory_space=pltpu.VMEM)
    shape = lambda b: (pieces, 2, (cols >> b + 1) * part, chunk)
    pairs = amplitudes.reshape(occ, 2, tiles, TILE).transpose(0, 2, 1, 3).reshape(occ * tiles * 2, TILE)
    out = pl.pallas_call(
        functools.partial(kernel, (rows, cols, groups, per_row, part, tiles, ab_tiles, early)),
        out_shape=jax.ShapeDtypeStruct((own * ab_tiles * 2, TILE), F32),
        in_specs=[pl.BlockSpec(memory_space=pl.ANY), vmem, pl.BlockSpec(memory_space=pltpu.SMEM),
                  pl.BlockSpec(memory_space=pl.ANY)],
        out_specs=vmem,
        scratch_shapes=[
            pltpu.VMEM((occ * tiles * 2, TILE), F32),
            pltpu.VMEM((chunks, 2, cd_width, chunk), BF16),
            pltpu.VMEM((part, cd_width), BF16),
            pltpu.VMEM((part, cd_width), BF16),
            pltpu.VMEM((max(flips - 1, 1), part, cd_width), F32),
            pltpu.VMEM((max(flips - 1, 1), part, cd_width), F32),
            pltpu.VMEM((groups, 2, cols, part, cd_width), BF16),
            pltpu.VMEM(shape(0), F32),
            pltpu.VMEM((ab_tiles, TILE), jnp.int32),
        ] + [pltpu.VMEM(shape(b), BF16) for b in range(col_bits)] * 2 + [
            pltpu.VMEM((pieces, part, chunk), F32),
            pltpu.VMEM((pieces, part, chunk), F32),
            pltpu.SemaphoreType.DMA((1,)),
            pltpu.SemaphoreType.DMA((chunks, 2)),
            pltpu.SemaphoreType.DMA((2, flips)),
            pltpu.SemaphoreType.DMA((2, groups * rows * per_row)),
            pltpu.SemaphoreType.DMA((2, col_bits, pieces)),
            pltpu.SemaphoreType.DMA((2, pieces)),
        ],
        compiler_params=pltpu.CompilerParams(
            collective_id=0, has_side_effects=True, vmem_limit_bytes=60 * 1024 * 1024),
    )(pairs, mirror.reshape(-1, TILE), screen, integrals)
    residual = out.reshape(own, ab_tiles, 2, TILE).transpose(0, 2, 1, 3).reshape(own, 2, ab_width)
    return residual / denominators


def solution(mesh):
    in_specs = (
        P("row", None, "col"),
        P(None, "col", "row"),
        P(None, "col", "row"),
        P(),
        P("col", None, "row"),
    )
    out_specs = P("col", None, "row")
    return jax.shard_map(body, mesh=mesh, in_specs=in_specs, out_specs=out_specs, check_vma=False)
```

```python
import functools

import jax
import jax.numpy as jnp
from jax import lax
from jax.experimental import pallas as pl
from jax.experimental.pallas import tpu as pltpu
from jax.sharding import PartitionSpec as P

TILE = 128
CHUNK = 512
LAGS = (3, 3, 3)
F32, BF16 = jnp.float32, jnp.bfloat16


def flip(x, bits):
    result = x
    place = 0
    while bits >> place:
        if bits >> place & 1:
            result = result + (1 - 2 * (x // (1 << place) % 2)) * (1 << place)
        place += 1
    return result


def position(owner, me, bits):
    total = 0
    for i in range(bits):
        differs = (owner // (1 << i) + me // (1 << i)) % 2
        total = total + differs * (1 << (bits - 1 - i))
    return total


def kernel(sizes, amps, mirror, screen, integrals, out,
           loaded, held, away_src, away_dst, flip_src, flip_dst, signed, acc, inverse, *rest):
    rows, cols, groups, per_row, part, tiles, ab_tiles, early = sizes
    row_bits, col_bits = rows.bit_length() - 1, cols.bit_length() - 1
    sends, recvs = rest[:col_bits], rest[col_bits:2 * col_bits]
    msend, mrecv, a_sem, k_sem, f_sem, g_sem, r_sem, m_sem = rest[2 * col_bits:]
    cd_width = tiles * TILE
    chunk = held.shape[-1]
    lanes = chunk // TILE
    chunks = ab_tiles // lanes
    pieces = groups * chunks
    row_me, col_me = lax.axis_index("row"), lax.axis_index("col")
    half = cols * part // 2

    def a_copy():
        return pltpu.make_async_copy(amps, loaded, a_sem.at[0])

    def k_copy(c, s):
        return pltpu.make_async_copy(
            integrals.at[s, :, pl.ds(pl.multiple_of(c * chunk, chunk), chunk)], held.at[c, s], k_sem.at[c, s])

    def start_k(c, carry):
        for s in range(2):
            k_copy(c, s).start()
        return carry

    a_copy().start()
    lax.fori_loop(0, chunks, start_k, 0)

    barrier = pltpu.get_barrier_semaphore()
    for b in range(col_bits):
        pl.semaphore_signal(barrier, inc=1, device_id={"col": flip(col_me, 1 << b)}, device_id_type=pl.DeviceIdType.MESH)
    for b in range(row_bits):
        pl.semaphore_signal(barrier, inc=1, device_id={"row": flip(row_me, 1 << b)}, device_id_type=pl.DeviceIdType.MESH)

    def remote(src, dst, sem, target):
        return pltpu.make_async_remote_copy(
            src_ref=src, dst_ref=dst, send_sem=sem[0], recv_sem=sem[1],
            device_id=target, device_id_type=pl.DeviceIdType.MESH)

    flips = [(g, k) for g in range(groups) for k in reversed(range(per_row))]

    def member(k):
        total = 0
        for i in range(per_row.bit_length() - 1):
            total = total + (k // (1 << i) % 2 + col_me // (1 << i)) % 2 * (1 << i)
        return total

    def amp_rows(g, k, t, which):
        first = (member(k) * groups + g) * part
        return loaded[pl.ds(first * (2 * tiles) + 2 * t + which, part, stride=2 * tiles), :]

    def f_copy(n):
        src, dst = (away_src, away_dst) if n == 0 else (flip_src.at[n - 1], flip_dst.at[n - 1])
        return remote(src, dst, (f_sem.at[0, n], f_sem.at[1, n]), {"col": flip(col_me, cols // 2)})

    def stage_flip(n):
        g, k = flips[n]
        for t in range(tiles):
            at = pl.ds(t * TILE, TILE)
            value = amp_rows(g, k, t, 1)
            if n == 0:
                away_src[:, at] = value.astype(BF16)
            else:
                flip_src[n - 1, :, at] = value

    def gather_copies(g, stage, k):
        bit = row_bits - 1 - stage
        copies = []
        for t in range(1 << stage):
            shard = flip(row_me, t << (bit + 1))
            pos = position(shard * per_row + member(k), col_me, col_bits)
            i = (g * rows + (1 << stage) - 1 + t) * per_row + k
            block = signed.at[g, :, pos]
            copies.append(remote(block, block, (g_sem.at[0, i], g_sem.at[1, i]), {"row": flip(row_me, 1 << bit)}))
        return copies

    def gather_start(g, stage, k):
        for copy in gather_copies(g, stage, k):
            copy.start()

    def gather_wait(g, stage, k):
        for copy in gather_copies(g, stage, k):
            copy.wait()

    def make_signed(n):
        g, k = flips[n]
        f_copy(n).wait_recv()
        if n + 1 < len(flips):
            f_copy(n + 1).start()
        pos = position(row_me * per_row + member(k), col_me, col_bits)
        for t in range(tiles):
            at = pl.ds(t * TILE, TILE)
            index = jnp.broadcast_to(mirror[pl.ds(col_me * tiles + t, 1), :] % TILE, (part, TILE))
            arrived = away_dst[:, at].astype(F32) if n == 0 else flip_dst[n - 1, :, at]
            flipped = jnp.take_along_axis(arrived, index, axis=1)
            mine = amp_rows(g, k, t, 0)
            signed[g, 0, pos, :, at] = (mine + flipped).astype(BF16)
            signed[g, 1, pos, :, at] = (mine - flipped).astype(BF16)

    def keep_tiles(c):
        for s in range(2):
            k_copy(c, s).wait()

            def one(t, carry):
                for l in range(lanes):
                    factor = jnp.full((16, TILE), screen[s, t, c * lanes + l]).astype(F32).astype(BF16)
                    at = (c, s, pl.ds(pl.multiple_of(t * TILE, TILE), TILE), pl.ds(l * TILE, TILE))
                    block = held[at].reshape(TILE // 16, 16, TILE)
                    held[at] = (block * factor[None]).reshape(TILE, TILE)
                return carry

            lax.fori_loop(0, tiles, one, 0)

    def keep_range(lo, hi):
        def one(c, carry):
            keep_tiles(c)
            return carry

        if hi > lo:
            lax.fori_loop(lo, hi, one, 0)

    def invert(t, carry):
        index = jnp.broadcast_to(mirror[pl.ds(row_me * ab_tiles + t, 1), :] % TILE, (TILE, TILE))
        hit = jnp.where(lax.broadcasted_iota(jnp.int32, (TILE, TILE), 0) == index, 1.0, 0.0).astype(BF16)
        places = lax.broadcasted_iota(jnp.int32, (16, TILE), 1).astype(F32).astype(BF16)
        found = lax.dot_general(places, hit, (((1,), (1,)), ((), ())), preferred_element_type=F32)
        inverse[pl.ds(t, 1), :] = found[:1].astype(jnp.int32)
        return carry

    def stage_copy(b, q):
        return remote(sends[b].at[q], recvs[b].at[q], (r_sem.at[0, b, q], r_sem.at[1, b, q]),
                      {"col": flip(col_me, 1 << b)})

    def mirror_copy(q):
        return remote(msend.at[q], mrecv.at[q], (m_sem.at[0, q], m_sem.at[1, q]),
                      {"row": flip(row_me, rows // 2)})

    def multiply_away(q, carry):
        for s in range(2):
            lhs = signed[0, s, cols // 2:].reshape(half, cd_width)
            sends[0][q, s] = jnp.dot(lhs, held[q, s], preferred_element_type=F32).astype(BF16)
        stage_copy(0, q).start()
        return carry

    def multiply_own(q, carry):
        for s in range(2):
            lhs = signed[0, s, :cols // 2].reshape(half, cd_width)
            acc[q, s] = jnp.dot(lhs, held[q, s], preferred_element_type=F32)
        return carry

    def multiply(q):
        g, c = q // chunks, q % chunks
        for s in range(2):
            lhs = signed[g, s].reshape(cols * part, cd_width)
            total = jnp.dot(lhs, held[c, s], preferred_element_type=F32)
            sends[0][q, s] = total[half:].astype(BF16)
            acc[q, s] = total[:half]
        stage_copy(0, q).start()

    def reduce(b, q):
        stage_copy(b - 1, q).wait()
        few = (cols >> b) * part // 2
        for s in range(2):
            sends[b][q, s] = (acc[q, s, few:2 * few] + recvs[b - 1][q, s, few:2 * few].astype(F32)).astype(BF16)
        stage_copy(b, q).start()
        for s in range(2):
            acc[q, s, :few] = acc[q, s, :few] + recvs[b - 1][q, s, :few].astype(F32)

    def out_rows(q, l, which):
        g, c = q // chunks, q % chunks
        return pl.ds(g * (part * 2 * ab_tiles) + 2 * (c * lanes + l) + which, part, stride=2 * ab_tiles)

    def combine(q):
        c = q % chunks
        stage_copy(col_bits - 1, q).wait()
        for l in range(lanes):
            at = pl.ds(l * TILE, TILE)
            plus = acc[q, 0, :part, at] + recvs[-1][q, 0, :, at].astype(F32)
            minus = acc[q, 1, :part, at] + recvs[-1][q, 1, :, at].astype(F32)
            index = jnp.broadcast_to(inverse[pl.ds(c * lanes + l, 1), :], (part, TILE))
            msend[q, :, at] = jnp.take_along_axis(0.5 * (plus - minus), index, axis=1)
            out[out_rows(q, l, 0), :] = 0.5 * (plus + minus)
        mirror_copy(q).start()

    def place(q):
        mirror_copy(q).wait()
        for l in range(lanes):
            out[out_rows(q, l, 1), :] = mrecv[q, :, pl.ds(l * TILE, TILE)]

    a_copy().wait()
    stage_flip(0)
    pl.semaphore_wait(barrier, col_bits + row_bits)
    f_copy(0).start()
    for n in range(1, len(flips)):
        stage_flip(n)

    cut = lambda x: chunks * x // 8
    keep_range(0, cut(3))
    make_signed(0)
    gather_start(0, 0, per_row - 1)
    keep_range(cut(3), cut(6))
    for stage in range(1, row_bits):
        gather_wait(0, stage - 1, per_row - 1)
        gather_start(0, stage, per_row - 1)
    keep_range(cut(6), chunks)
    gather_wait(0, row_bits - 1, per_row - 1)
    for k in reversed(range(1, per_row - 1)):
        make_signed(per_row - 1 - k)
        for stage in range(row_bits):
            gather_start(0, stage, k)
            gather_wait(0, stage, k)
    if per_row > 1:
        lax.fori_loop(0, early // 2, multiply_away, 0)
        make_signed(per_row - 1)
        gather_start(0, 0, 0)
        lax.fori_loop(0, ab_tiles, invert, 0)
        lax.fori_loop(early // 2, early, multiply_away, 0)
        for stage in range(1, row_bits):
            gather_wait(0, stage - 1, 0)
            gather_start(0, stage, 0)
        gather_wait(0, row_bits - 1, 0)
        lax.fori_loop(0, early, multiply_own, 0)

    start = min(early, LAGS[0])
    events = []
    for g in range(1, groups):
        last = g * chunks
        first = g * per_row
        for k in reversed(range(per_row)):
            n = first + per_row - 1 - k
            begin = max(last - 1 - 3 * k, start)
            events.append((begin, functools.partial(make_signed, n)))
            for stage in range(row_bits):
                if stage:
                    events.append((min(begin + stage, last), functools.partial(gather_wait, g, stage - 1, k)))
                events.append((min(begin + stage, last), functools.partial(gather_start, g, stage, k)))
            events.append((last, functools.partial(gather_wait, g, row_bits - 1, k)))

    def step(i, carry):
        for when in sorted(set(w for w, _ in events)):
            @pl.when(i == when)
            def _():
                for w, action in events:
                    if w == when:
                        action()

        @pl.when((i >= early) & (i < pieces))
        def _():
            multiply(i)

        lag = 0
        for b in range(1, col_bits):
            lag += LAGS[min(b - 1, 1)]

            @pl.when((i >= lag) & (i < pieces + lag))
            def _():
                reduce(b, i - lag)

        lag += LAGS[1]

        @pl.when((i >= lag) & (i < pieces + lag))
        def _():
            combine(i - lag)

        lag += LAGS[2]

        @pl.when((i >= lag) & (i < pieces + lag))
        def _():
            place(i - lag)

        return carry

    lax.fori_loop(start, pieces + LAGS[0] + (col_bits - 1) * LAGS[1] + LAGS[2], step, 0)
    for n in range(len(flips)):
        f_copy(n).wait_send()


def body(amplitudes, integrals, screen, mirror, denominators):
    cols, rows = lax.axis_size("col"), lax.axis_size("row")
    col_bits = cols.bit_length() - 1
    occ, _, cd_width = amplitudes.shape
    own, _, ab_width = denominators.shape
    per_row = occ // own
    groups = 2 if own % 32 == 0 else 1
    part = own // groups
    chunk = min(CHUNK, ab_width)
    chunks = ab_width // chunk
    pieces = groups * chunks
    tiles, ab_tiles = cd_width // TILE, ab_width // TILE
    early = min(4, chunks) if per_row > 1 else 0
    flips = groups * per_row
    vmem = pl.BlockSpec(memory_space=pltpu.VMEM)
    shape = lambda b: (pieces, 2, (cols >> b + 1) * part, chunk)
    pairs = amplitudes.reshape(occ, 2, tiles, TILE).transpose(0, 2, 1, 3).reshape(occ * tiles * 2, TILE)
    out = pl.pallas_call(
        functools.partial(kernel, (rows, cols, groups, per_row, part, tiles, ab_tiles, early)),
        out_shape=jax.ShapeDtypeStruct((own * ab_tiles * 2, TILE), F32),
        in_specs=[pl.BlockSpec(memory_space=pl.ANY), vmem, pl.BlockSpec(memory_space=pltpu.SMEM),
                  pl.BlockSpec(memory_space=pl.ANY)],
        out_specs=vmem,
        scratch_shapes=[
            pltpu.VMEM((occ * tiles * 2, TILE), F32),
            pltpu.VMEM((chunks, 2, cd_width, chunk), BF16),
            pltpu.VMEM((part, cd_width), BF16),
            pltpu.VMEM((part, cd_width), BF16),
            pltpu.VMEM((max(flips - 1, 1), part, cd_width), F32),
            pltpu.VMEM((max(flips - 1, 1), part, cd_width), F32),
            pltpu.VMEM((groups, 2, cols, part, cd_width), BF16),
            pltpu.VMEM(shape(0), F32),
            pltpu.VMEM((ab_tiles, TILE), jnp.int32),
        ] + [pltpu.VMEM(shape(b), BF16) for b in range(col_bits)] * 2 + [
            pltpu.VMEM((pieces, part, chunk), F32),
            pltpu.VMEM((pieces, part, chunk), F32),
            pltpu.SemaphoreType.DMA((1,)),
            pltpu.SemaphoreType.DMA((chunks, 2)),
            pltpu.SemaphoreType.DMA((2, flips)),
            pltpu.SemaphoreType.DMA((2, groups * rows * per_row)),
            pltpu.SemaphoreType.DMA((2, col_bits, pieces)),
            pltpu.SemaphoreType.DMA((2, pieces)),
        ],
        compiler_params=pltpu.CompilerParams(
            collective_id=0, has_side_effects=True, vmem_limit_bytes=60 * 1024 * 1024),
    )(pairs, mirror.reshape(-1, TILE), screen, integrals)
    divisors = denominators.reshape(own, 2, ab_tiles, TILE).transpose(0, 2, 1, 3).reshape(own * ab_tiles * 2, TILE)
    update = out / divisors
    return update.reshape(own, ab_tiles, 2, TILE).transpose(0, 2, 1, 3).reshape(own, 2, ab_width)


def solution(mesh):
    in_specs = (
        P("row", None, "col"),
        P(None, "col", "row"),
        P(None, "col", "row"),
        P(),
        P("col", None, "row"),
    )
    out_specs = P("col", None, "row")
    return jax.shard_map(body, mesh=mesh, in_specs=in_specs, out_specs=out_specs, check_vma=False)
```

```python
import functools

import jax
import jax.numpy as jnp
from jax import lax
from jax.experimental import pallas as pl
from jax.experimental.pallas import tpu as pltpu
from jax.sharding import PartitionSpec as P

TILE = 128
CHUNK = 512
LAGS = (3, 3, 3)
NEAR = 2
FOLLOW = {}
KEEPS = (3, 4, 6)
EARLY = (4, 2)
UNROLL = 8
EVENTS = (1, 3)
SPARE = (1, 1, 4)
F32, BF16 = jnp.float32, jnp.bfloat16


def flip(x, bits):
    result = x
    place = 0
    while bits >> place:
        if bits >> place & 1:
            result = result + (1 - 2 * (x // (1 << place) % 2)) * (1 << place)
        place += 1
    return result


def position(owner, me, bits):
    total = 0
    for i in range(bits):
        differs = (owner // (1 << i) + me // (1 << i)) % 2
        total = total + differs * (1 << (bits - 1 - i))
    return total


def kernel(sizes, amps, mirror, screen, integrals, out,
           loaded, held, near_src, near_dst, flip_src, flip_dst, signed, acc, inverse, *rest):
    rows, cols, groups, per_row, part, tiles, ab_tiles, early, split, spare = sizes
    row_bits, col_bits = rows.bit_length() - 1, cols.bit_length() - 1
    sends, recvs = rest[:col_bits], rest[col_bits:2 * col_bits]
    rest = rest[2 * col_bits:]
    msend, mrecv, a_sem, k_sem, f_sem, g_sem, r_sem, m_sem = rest[:8]
    rest = rest[8:]
    if spare:
        s_sem, s_acc, s_sends, s_recvs = rest[0], rest[1], rest[2:2 + col_bits], rest[2 + col_bits:]
    cd_width = tiles * TILE
    chunk = held.shape[-1]
    lanes = chunk // TILE
    chunks = ab_tiles // lanes
    pieces = groups * chunks
    row_me, col_me = lax.axis_index("row"), lax.axis_index("col")
    half = cols * part // 2
    classes = rows // 2
    ordinary = pieces - spare

    def a_copy():
        return pltpu.make_async_copy(amps, loaded, a_sem.at[0])

    def k_copy(c, s):
        return pltpu.make_async_copy(
            integrals.at[s, :, pl.ds(pl.multiple_of(c * chunk, chunk), chunk)], held.at[c, s], k_sem.at[c, s])

    def start_k(c, carry):
        for s in range(2):
            k_copy(c, s).start()
        return carry

    a_copy().start()
    lax.fori_loop(0, chunks, start_k, 0)

    barrier = pltpu.get_barrier_semaphore()
    for b in range(col_bits):
        pl.semaphore_signal(barrier, inc=1, device_id={"col": flip(col_me, 1 << b)}, device_id_type=pl.DeviceIdType.MESH)
    for b in range(row_bits):
        pl.semaphore_signal(barrier, inc=1, device_id={"row": flip(row_me, 1 << b)}, device_id_type=pl.DeviceIdType.MESH)

    def remote(src, dst, sem, target):
        return pltpu.make_async_remote_copy(
            src_ref=src, dst_ref=dst, send_sem=sem[0], recv_sem=sem[1],
            device_id=target, device_id_type=pl.DeviceIdType.MESH)

    flips = [(g, k) for g in range(groups) for k in reversed(range(per_row))]

    def member(k):
        total = 0
        for i in range(per_row.bit_length() - 1):
            total = total + (k // (1 << i) % 2 + col_me // (1 << i)) % 2 * (1 << i)
        return total

    def amp_rows(g, k, t, which):
        first = (member(k) * groups + g) * part
        return loaded[pl.ds(first * (2 * tiles) + 2 * t + which, part, stride=2 * tiles), :]

    def f_copy(n):
        src, dst = (near_src.at[n], near_dst.at[n]) if n < NEAR else (flip_src.at[n - NEAR], flip_dst.at[n - NEAR])
        return remote(src, dst, (f_sem.at[0, n], f_sem.at[1, n]), {"col": flip(col_me, cols // 2)})

    def stage_flip(n):
        g, k = flips[n]
        for t in range(tiles):
            at = pl.ds(t * TILE, TILE)
            value = amp_rows(g, k, t, 1)
            if n < NEAR:
                near_src[n, :, at] = value.astype(BF16)
            else:
                flip_src[n - NEAR, :, at] = value

    def place_of(shard):
        return position(shard, col_me // per_row, row_bits)

    def gather_copy(g, stage, k, t):
        bit = row_bits - 1 - stage
        pos = place_of(flip(row_me, t << (bit + 1)))
        i = (g * rows + (1 << stage) - 1 + t) * per_row + k
        block = signed.at[g, :, k, pos // classes, pos % classes]
        return remote(block, block, (g_sem.at[0, i], g_sem.at[1, i]), {"row": flip(row_me, 1 << bit)})

    def gather_first(g, k):
        for stage in range(row_bits):
            gather_copy(g, stage, k, 0).start()

    def gather_core(g, k):
        gather_copy(g, row_bits - 1, k, 0).wait()

    def gather_next(g, stage, k):
        final = stage == row_bits - 1
        for t in range(1 if final else 0, 1 << stage):
            gather_copy(g, stage, k, t).wait()
        if not final:
            for t in range(1, 2 << stage):
                gather_copy(g, stage + 1, k, t).start()

    def make_signed(n):
        g, k = flips[n]
        f_copy(n).wait_recv()
        for later in FOLLOW.get(n, (n + 1,)):
            if later < len(flips):
                f_copy(later).start()
        pos = place_of(row_me)
        for t in range(tiles):
            at = pl.ds(t * TILE, TILE)
            index = jnp.broadcast_to(mirror[pl.ds(col_me * tiles + t, 1), :] % TILE, (part, TILE))
            arrived = near_dst[n, :, at].astype(F32) if n < NEAR else flip_dst[n - NEAR, :, at]
            flipped = jnp.take_along_axis(arrived, index, axis=1)
            mine = amp_rows(g, k, t, 0)
            signed[g, 0, k, pos // classes, pos % classes, :, at] = (mine + flipped).astype(BF16)
            signed[g, 1, k, pos // classes, pos % classes, :, at] = (mine - flipped).astype(BF16)

    def keep_tiles(c):
        for s in range(2):
            k_copy(c, s).wait()

            def one(t, carry):
                for l in range(lanes):
                    factor = jnp.full((16, TILE), screen[s, t, c * lanes + l]).astype(F32).astype(BF16)
                    at = (c, s, pl.ds(pl.multiple_of(t * TILE, TILE), TILE), pl.ds(l * TILE, TILE))
                    block = held[at].reshape(TILE // 16, 16, TILE)
                    held[at] = (block * factor[None]).reshape(TILE, TILE)
                return carry

            lax.fori_loop(0, tiles, one, 0)

    def keep_range(lo, hi):
        def one(c, carry):
            keep_tiles(c)
            return carry

        if hi > lo:
            lax.fori_loop(lo, hi, one, 0)

    def invert(t, carry):
        index = jnp.broadcast_to(mirror[pl.ds(row_me * ab_tiles + t, 1), :] % TILE, (TILE, TILE))
        hit = jnp.where(lax.broadcasted_iota(jnp.int32, (TILE, TILE), 0) == index, 1.0, 0.0).astype(BF16)
        places = lax.broadcasted_iota(jnp.int32, (16, TILE), 1).astype(F32).astype(BF16)
        found = lax.dot_general(places, hit, (((1,), (1,)), ((), ())), preferred_element_type=F32)
        inverse[pl.ds(t, 1), :] = found[:1].astype(jnp.int32)
        return carry

    def stage_copy(b, q):
        return remote(sends[b].at[q], recvs[b].at[q], (r_sem.at[0, b, q], r_sem.at[1, b, q]),
                      {"col": flip(col_me, 1 << b)})

    def mirror_copy(q):
        return remote(msend.at[q], mrecv.at[q], (m_sem.at[0, q], m_sem.at[1, q]),
                      {"row": flip(row_me, rows // 2)})

    def early_copy(q, a):
        return remote(sends[0].at[q, :, :, a], recvs[0].at[q, :, :, a], (r_sem.at[0, 0, q], r_sem.at[1, 0, q]),
                      {"col": flip(col_me, 1)})

    def multiply_away(j, q, carry):
        a = flip(place_of(row_me) % classes, j)
        for s in range(2):
            lhs = signed[0, s, per_row - 1, :, a].reshape(2 * part, cd_width)
            total = jnp.dot(lhs, held[q, s], preferred_element_type=F32).astype(BF16)
            sends[0][q, s, :, a] = total.reshape(2, part, chunk)
        early_copy(q, a).start()
        return carry

    def multiply_leaving(q, carry):
        for s in range(2):
            lhs = signed[0, s, per_row - 1].reshape(half, cd_width)
            total = jnp.dot(lhs, held[q, s], preferred_element_type=F32).astype(BF16)
            sends[0][q, s] = total.reshape(2, classes, part, chunk)
        stage_copy(0, q).start()
        return carry

    def multiply_own(q, carry):
        for s in range(2):
            lhs = signed[0, s, 0].reshape(half, cd_width)
            acc[q, s] = jnp.dot(lhs, held[q, s], preferred_element_type=F32)
        return carry

    def multiply(q):
        g, c = q // chunks, q % chunks
        for s in range(2):
            lhs = signed[g, s].reshape(cols * part, cd_width)
            total = jnp.dot(lhs, held[c, s], preferred_element_type=F32)
            sends[0][q, s] = total[half:].astype(BF16).reshape(2, classes, part, chunk)
            acc[q, s] = total[:half]
        stage_copy(0, q).start()

    def received(b, q, s, lo, hi):
        if b:
            return recvs[b][q, s, lo * part:hi * part].astype(F32)
        lo, hi = lo // classes, max(hi // classes, 1)
        return recvs[b][q, s, lo:hi].reshape((hi - lo) * classes * part, chunk).astype(F32)

    def reduce(b, q):
        stage_copy(b - 1, q).wait()
        few = (cols >> b) // 2
        for s in range(2):
            sends[b][q, s] = (acc[q, s, few * part:2 * few * part] + received(b - 1, q, s, few, 2 * few)).astype(BF16)
        stage_copy(b, q).start()
        for s in range(2):
            acc[q, s, :few * part] = acc[q, s, :few * part] + received(b - 1, q, s, 0, few)

    order = list(range(1, col_bits)) + [0]

    def chosen(done, bit, which):
        return tuple(0 if d in done else which if d == bit else slice(None) for d in range(col_bits))

    def spare_copy(j, u):
        return remote(s_sends[j].at[u], s_recvs[j].at[u], (s_sem.at[0, j, u], s_sem.at[1, j, u]),
                      {"col": flip(col_me, 1 << order[j])})

    def spare_multiply(u):
        c = chunks - spare + u
        for s in range(2):
            lhs = signed[groups - 1, s].reshape(cols * part, cd_width)
            total = jnp.dot(lhs, held[c, s], preferred_element_type=F32).reshape((2,) * col_bits + (part, chunk))
            s_acc[u, s] = total
            s_sends[0][u, s] = total[chosen((), order[0], 1)].astype(BF16)
        spare_copy(0, u).start()

    def spare_reduce(j, u):
        spare_copy(j - 1, u).wait()
        left = [d for d in range(col_bits) if d not in order[:j]]
        for s in range(2):
            kept = s_acc[(u, s) + chosen(order[:j], None, 0)] + s_recvs[j - 1][u, s].astype(F32)
            pick = lambda which: tuple(which if d == order[j] else slice(None) for d in left)
            s_sends[j][u, s] = kept[pick(1)].astype(BF16)
            s_acc[(u, s) + chosen(order[:j], order[j], 0)] = kept[pick(0)]
        spare_copy(j, u).start()

    def spare_combine(u):
        spare_copy(col_bits - 1, u).wait()
        kept = [s_acc[(u, s) + (0,) * col_bits] + s_recvs[-1][u, s].astype(F32) for s in range(2)]
        finish(ordinary + u, kept)

    def out_rows(q, l, which):
        g, c = q // chunks, q % chunks
        return pl.ds(g * (part * 2 * ab_tiles) + 2 * (c * lanes + l) + which, part, stride=2 * ab_tiles)

    def finish(q, kept):
        for l in range(lanes):
            plus, minus = (x[:, l * TILE:(l + 1) * TILE] for x in kept)
            at = pl.ds(l * TILE, TILE)
            index = jnp.broadcast_to(inverse[pl.ds(q % chunks * lanes + l, 1), :], (part, TILE))
            msend[q, :, at] = jnp.take_along_axis(0.5 * (plus - minus), index, axis=1)
            out[out_rows(q, l, 0), :] = 0.5 * (plus + minus)
        mirror_copy(q).start()

    def combine(q):
        stage_copy(col_bits - 1, q).wait()
        finish(q, [acc[q, s, :part] + recvs[-1][q, s].astype(F32) for s in range(2)])

    def place(q):
        mirror_copy(q).wait()
        for l in range(lanes):
            out[out_rows(q, l, 1), :] = mrecv[q, :, pl.ds(l * TILE, TILE)]

    a_copy().wait()
    stage_flip(0)
    pl.semaphore_wait(barrier, col_bits + row_bits)
    f_copy(0).start()
    for n in range(1, len(flips)):
        stage_flip(n)

    cut = lambda x: chunks * x // 8
    lax.fori_loop(0, ab_tiles, invert, 0, unroll=UNROLL)
    keep_range(0, cut(KEEPS[0]))
    make_signed(0)
    gather_first(0, 1)
    keep_range(cut(KEEPS[0]), cut(KEEPS[1]))
    gather_core(0, 1)
    lax.fori_loop(0, split, functools.partial(multiply_away, 0), 0)
    if row_bits > 1:
        gather_next(0, 0, 1)
    keep_range(cut(KEEPS[1]), cut(KEEPS[2]))
    make_signed(1)
    gather_first(0, 0)
    for stage in range(1, row_bits):
        gather_next(0, stage, 1)
    for a in range(1, classes):
        lax.fori_loop(0, split, functools.partial(multiply_away, a), 0)
    lax.fori_loop(split, early, multiply_leaving, 0)
    for stage in range(row_bits - 1):
        gather_next(0, stage, 0)
    keep_range(cut(KEEPS[2]), chunks)
    gather_core(0, 0)
    gather_next(0, row_bits - 1, 0)
    lax.fori_loop(0, early, multiply_own, 0)

    start = min(early, LAGS[0])
    events, after = [], []
    for g in range(1, groups):
        last = g * chunks
        for k in reversed(range(per_row)):
            begin = max(last - EVENTS[0] - EVENTS[1] * k, start)
            events.append((begin, functools.partial(make_signed, (g + 1) * per_row - 1 - k)))
            events.append((begin, functools.partial(gather_first, g, k)))
            for stage in range(row_bits - 1):
                events.append((min(begin + stage + 1, last), functools.partial(gather_next, g, stage, k)))
            events.append((last, functools.partial(gather_core, g, k)))
            events.append((last, functools.partial(gather_next, g, row_bits - 1, k)))
    for u in range(spare):
        begin = (groups - 1) * chunks + SPARE[1] + u
        late = [(begin, functools.partial(spare_multiply, u))]
        for j in range(1, col_bits):
            late.append((begin + SPARE[2] * j, functools.partial(spare_reduce, j, u)))
        late.append((begin + SPARE[2] * col_bits, functools.partial(spare_combine, u)))
        late.append((begin + SPARE[2] * col_bits + LAGS[2], functools.partial(place, ordinary + u)))
        after.extend(late)
    end = max([ordinary + LAGS[0] + (col_bits - 1) * LAGS[1] + LAGS[2]] + [w + 1 for w, _ in after])

    def act(i, listed):
        for when in sorted(set(w for w, _ in listed)):
            @pl.when(i == when)
            def _():
                for w, action in listed:
                    if w == when:
                        action()

    def step(i, carry):
        act(i, events)

        @pl.when((i >= early) & (i < ordinary))
        def _():
            multiply(i)

        lag = 0
        for b in range(1, col_bits):
            lag += LAGS[min(b - 1, 1)]

            @pl.when((i >= lag) & (i < ordinary + lag))
            def _():
                reduce(b, i - lag)

        lag += LAGS[1]

        @pl.when((i >= lag) & (i < ordinary + lag))
        def _():
            combine(i - lag)

        lag += LAGS[2]

        @pl.when((i >= lag) & (i < ordinary + lag))
        def _():
            place(i - lag)

        act(i, after)
        return carry

    lax.fori_loop(start, end, step, 0)
    for n in range(len(flips)):
        f_copy(n).wait_send()


def body(amplitudes, integrals, screen, mirror, denominators):
    cols, rows = lax.axis_size("col"), lax.axis_size("row")
    col_bits = cols.bit_length() - 1
    occ, _, cd_width = amplitudes.shape
    own, _, ab_width = denominators.shape
    per_row = occ // own
    groups = 2 if own % 32 == 0 else 1
    part = own // groups
    chunk = min(CHUNK, ab_width)
    chunks = ab_width // chunk
    pieces = groups * chunks
    tiles, ab_tiles = cd_width // TILE, ab_width // TILE
    early, split = min(EARLY[0], chunks), min(EARLY[1], chunks)
    spare = SPARE[0] if pieces >= 16 else 0
    flips = groups * per_row
    far = max(flips - NEAR, 1)
    vmem = pl.BlockSpec(memory_space=pltpu.VMEM)
    shape = lambda b: (pieces, 2, (cols >> b + 1) * part, chunk)
    pairs = amplitudes.reshape(occ, 2, tiles, TILE).transpose(0, 2, 1, 3).reshape(occ * tiles * 2, TILE)
    out = pl.pallas_call(
        functools.partial(kernel, (rows, cols, groups, per_row, part, tiles, ab_tiles, early, split, spare)),
        out_shape=jax.ShapeDtypeStruct((own * ab_tiles * 2, TILE), F32),
        in_specs=[pl.BlockSpec(memory_space=pl.ANY), vmem, pl.BlockSpec(memory_space=pltpu.SMEM),
                  pl.BlockSpec(memory_space=pl.ANY)],
        out_specs=vmem,
        scratch_shapes=[
            pltpu.VMEM((occ * tiles * 2, TILE), F32),
            pltpu.VMEM((chunks, 2, cd_width, chunk), BF16),
            pltpu.VMEM((NEAR, part, cd_width), BF16),
            pltpu.VMEM((NEAR, part, cd_width), BF16),
            pltpu.VMEM((far, part, cd_width), F32),
            pltpu.VMEM((far, part, cd_width), F32),
            pltpu.VMEM((groups, 2, per_row, 2, rows // 2, part, cd_width), BF16),
            pltpu.VMEM(shape(0), F32),
            pltpu.VMEM((ab_tiles, TILE), jnp.int32),
        ] + ([pltpu.VMEM((pieces, 2, 2, rows // 2, part, chunk), BF16)] + [pltpu.VMEM(shape(b), BF16) for b in range(1, col_bits)]) * 2 + [
            pltpu.VMEM((pieces, part, chunk), F32),
            pltpu.VMEM((pieces, part, chunk), F32),
            pltpu.SemaphoreType.DMA((1,)),
            pltpu.SemaphoreType.DMA((chunks, 2)),
            pltpu.SemaphoreType.DMA((2, flips)),
            pltpu.SemaphoreType.DMA((2, groups * rows * per_row)),
            pltpu.SemaphoreType.DMA((2, col_bits, pieces)),
            pltpu.SemaphoreType.DMA((2, pieces)),
        ] + ([
            pltpu.SemaphoreType.DMA((2, col_bits, spare)),
            pltpu.VMEM((spare, 2) + (2,) * col_bits + (part, chunk), F32),
        ] + [pltpu.VMEM((spare, 2) + (2,) * (col_bits - 1 - b) + (part, chunk), BF16) for b in range(col_bits)] * 2 if spare else []),
        compiler_params=pltpu.CompilerParams(
            collective_id=0, has_side_effects=True, vmem_limit_bytes=60 * 1024 * 1024),
    )(pairs, mirror.reshape(-1, TILE), screen, integrals)
    divisors = denominators.reshape(own, 2, ab_tiles, TILE).transpose(0, 2, 1, 3).reshape(own * ab_tiles * 2, TILE)
    update = out / divisors
    return update.reshape(own, ab_tiles, 2, TILE).transpose(0, 2, 1, 3).reshape(own, 2, ab_width)


def solution(mesh):
    in_specs = (
        P("row", None, "col"),
        P(None, "col", "row"),
        P(None, "col", "row"),
        P(),
        P("col", None, "row"),
    )
    out_specs = P("col", None, "row")
    return jax.shard_map(body, mesh=mesh, in_specs=in_specs, out_specs=out_specs, check_vma=False)
```

```python
import functools

import jax
import jax.numpy as jnp
from jax import lax
from jax.experimental import pallas as pl
from jax.experimental.pallas import tpu as pltpu
from jax.sharding import PartitionSpec as P

TILE = 128
CHUNK = 512
LAGS = (2, 3, 3)
NEAR = 2
FOLLOW = {}
KEEPS = (3, 4, 6)
EARLY = (4, 2)
UNROLL = 8
EVENTS = (1, 3)
SPARE = (1, 1, 4)
F32, BF16 = jnp.float32, jnp.bfloat16


def flip(x, bits):
    result = x
    place = 0
    while bits >> place:
        if bits >> place & 1:
            result = result + (1 - 2 * (x // (1 << place) % 2)) * (1 << place)
        place += 1
    return result


def position(owner, me, bits):
    total = 0
    for i in range(bits):
        differs = (owner // (1 << i) + me // (1 << i)) % 2
        total = total + differs * (1 << (bits - 1 - i))
    return total


def kernel(sizes, amps, mirror, screen, integrals, out,
           loaded, held, near_src, near_dst, flip_src, flip_dst, signed, acc, inverse, *rest):
    rows, cols, groups, per_row, part, tiles, ab_tiles, early, split, spare = sizes
    row_bits, col_bits = rows.bit_length() - 1, cols.bit_length() - 1
    sends, recvs = rest[:col_bits], rest[col_bits:2 * col_bits]
    rest = rest[2 * col_bits:]
    msend, mrecv, a_sem, k_sem, f_sem, g_sem, r_sem, m_sem = rest[:8]
    rest = rest[8:]
    if spare:
        s_sem, s_acc, s_sends, s_recvs = rest[0], rest[1], rest[2:2 + col_bits], rest[2 + col_bits:]
    cd_width = tiles * TILE
    chunk = held.shape[-1]
    lanes = chunk // TILE
    chunks = ab_tiles // lanes
    pieces = groups * chunks
    row_me, col_me = lax.axis_index("row"), lax.axis_index("col")
    half = cols * part // 2
    classes = rows // 2
    ordinary = pieces - spare

    def a_copy():
        return pltpu.make_async_copy(amps, loaded, a_sem.at[0])

    def k_copy(c, s):
        return pltpu.make_async_copy(
            integrals.at[s, :, pl.ds(pl.multiple_of(c * chunk, chunk), chunk)], held.at[c, s], k_sem.at[c, s])

    def start_k(c, carry):
        for s in range(2):
            k_copy(c, s).start()
        return carry

    a_copy().start()
    lax.fori_loop(0, chunks, start_k, 0)

    barrier = pltpu.get_barrier_semaphore()
    for b in range(col_bits):
        pl.semaphore_signal(barrier, inc=1, device_id={"col": flip(col_me, 1 << b)}, device_id_type=pl.DeviceIdType.MESH)
    for b in range(row_bits):
        pl.semaphore_signal(barrier, inc=1, device_id={"row": flip(row_me, 1 << b)}, device_id_type=pl.DeviceIdType.MESH)

    def remote(src, dst, sem, target):
        return pltpu.make_async_remote_copy(
            src_ref=src, dst_ref=dst, send_sem=sem[0], recv_sem=sem[1],
            device_id=target, device_id_type=pl.DeviceIdType.MESH)

    flips = [(g, k) for g in range(groups) for k in reversed(range(per_row))]

    def member(k):
        total = 0
        for i in range(per_row.bit_length() - 1):
            total = total + (k // (1 << i) % 2 + col_me // (1 << i)) % 2 * (1 << i)
        return total

    def amp_rows(g, k, t, which):
        first = (member(k) * groups + g) * part
        return loaded[pl.ds(first * (2 * tiles) + 2 * t + which, part, stride=2 * tiles), :]

    def f_copy(n):
        src, dst = (near_src.at[n], near_dst.at[n]) if n < NEAR else (flip_src.at[n - NEAR], flip_dst.at[n - NEAR])
        return remote(src, dst, (f_sem.at[0, n], f_sem.at[1, n]), {"col": flip(col_me, cols // 2)})

    def stage_flip(n):
        g, k = flips[n]
        for t in range(tiles):
            at = pl.ds(t * TILE, TILE)
            value = amp_rows(g, k, t, 1)
            if n < NEAR:
                near_src[n, :, at] = value.astype(BF16)
            else:
                flip_src[n - NEAR, :, at] = value

    def place_of(shard):
        return position(shard, col_me // per_row, row_bits)

    def gather_copy(g, stage, k, t):
        bit = row_bits - 1 - stage
        pos = place_of(flip(row_me, t << (bit + 1)))
        i = (g * rows + (1 << stage) - 1 + t) * per_row + k
        block = signed.at[g, :, k, pos // classes, pos % classes]
        return remote(block, block, (g_sem.at[0, i], g_sem.at[1, i]), {"row": flip(row_me, 1 << bit)})

    def gather_first(g, k):
        for stage in range(row_bits):
            gather_copy(g, stage, k, 0).start()

    def gather_core(g, k):
        gather_copy(g, row_bits - 1, k, 0).wait()

    def gather_next(g, stage, k):
        final = stage == row_bits - 1
        for t in range(1 if final else 0, 1 << stage):
            gather_copy(g, stage, k, t).wait()
        if not final:
            for t in range(1, 2 << stage):
                gather_copy(g, stage + 1, k, t).start()

    def make_signed(n):
        g, k = flips[n]
        f_copy(n).wait_recv()
        for later in FOLLOW.get(n, (n + 1,)):
            if later < len(flips):
                f_copy(later).start()
        pos = place_of(row_me)
        for t in range(tiles):
            at = pl.ds(t * TILE, TILE)
            index = jnp.broadcast_to(mirror[pl.ds(col_me * tiles + t, 1), :] % TILE, (part, TILE))
            arrived = near_dst[n, :, at].astype(F32) if n < NEAR else flip_dst[n - NEAR, :, at]
            flipped = jnp.take_along_axis(arrived, index, axis=1)
            mine = amp_rows(g, k, t, 0)
            signed[g, 0, k, pos // classes, pos % classes, :, at] = (mine + flipped).astype(BF16)
            signed[g, 1, k, pos // classes, pos % classes, :, at] = (mine - flipped).astype(BF16)

    def keep_tiles(c):
        for s in range(2):
            k_copy(c, s).wait()

            def one(t, carry):
                for l in range(lanes):
                    factor = jnp.full((16, TILE), screen[s, t, c * lanes + l]).astype(F32).astype(BF16)
                    at = (c, s, pl.ds(pl.multiple_of(t * TILE, TILE), TILE), pl.ds(l * TILE, TILE))
                    block = held[at].reshape(TILE // 16, 16, TILE)
                    held[at] = (block * factor[None]).reshape(TILE, TILE)
                return carry

            lax.fori_loop(0, tiles, one, 0)

    def keep_range(lo, hi):
        def one(c, carry):
            keep_tiles(c)
            return carry

        if hi > lo:
            lax.fori_loop(lo, hi, one, 0)

    def invert(t, carry):
        index = jnp.broadcast_to(mirror[pl.ds(row_me * ab_tiles + t, 1), :] % TILE, (TILE, TILE))
        hit = jnp.where(lax.broadcasted_iota(jnp.int32, (TILE, TILE), 0) == index, 1.0, 0.0).astype(BF16)
        places = lax.broadcasted_iota(jnp.int32, (16, TILE), 1).astype(F32).astype(BF16)
        found = lax.dot_general(places, hit, (((1,), (1,)), ((), ())), preferred_element_type=F32)
        inverse[pl.ds(t, 1), :] = found[:1].astype(jnp.int32)
        return carry

    def stage_copy(b, q):
        return remote(sends[b].at[q], recvs[b].at[q], (r_sem.at[0, b, q], r_sem.at[1, b, q]),
                      {"col": flip(col_me, 1 << b)})

    def mirror_copy(q):
        return remote(msend.at[q], mrecv.at[q], (m_sem.at[0, q], m_sem.at[1, q]),
                      {"row": flip(row_me, rows // 2)})

    def early_copy(q, a):
        return remote(sends[0].at[q, :, :, a], recvs[0].at[q, :, :, a], (r_sem.at[0, 0, q], r_sem.at[1, 0, q]),
                      {"col": flip(col_me, 1)})

    def multiply_away(j, q, carry):
        a = flip(place_of(row_me) % classes, j)
        for s in range(2):
            lhs = signed[0, s, per_row - 1, :, a].reshape(2 * part, cd_width)
            total = jnp.dot(lhs, held[q, s], preferred_element_type=F32).astype(BF16)
            sends[0][q, s, :, a] = total.reshape(2, part, chunk)
        early_copy(q, a).start()
        return carry

    def multiply_leaving(q, carry):
        for s in range(2):
            lhs = signed[0, s, per_row - 1].reshape(half, cd_width)
            total = jnp.dot(lhs, held[q, s], preferred_element_type=F32).astype(BF16)
            sends[0][q, s] = total.reshape(2, classes, part, chunk)
        stage_copy(0, q).start()
        return carry

    def multiply_own(q, carry):
        for s in range(2):
            lhs = signed[0, s, 0].reshape(half, cd_width)
            acc[q, s] = jnp.dot(lhs, held[q, s], preferred_element_type=F32)
        return carry

    def multiply(q):
        g, c = q // chunks, q % chunks
        for s in range(2):
            lhs = signed[g, s].reshape(cols * part, cd_width)
            total = jnp.dot(lhs, held[c, s], preferred_element_type=F32)
            sends[0][q, s] = total[half:].astype(BF16).reshape(2, classes, part, chunk)
            acc[q, s] = total[:half]
        stage_copy(0, q).start()

    def received(b, q, s, lo, hi):
        if b:
            return recvs[b][q, s, lo * part:hi * part].astype(F32)
        lo, hi = lo // classes, max(hi // classes, 1)
        return recvs[b][q, s, lo:hi].reshape((hi - lo) * classes * part, chunk).astype(F32)

    def reduce(b, q):
        stage_copy(b - 1, q).wait()
        few = (cols >> b) // 2
        for s in range(2):
            sends[b][q, s] = (acc[q, s, few * part:2 * few * part] + received(b - 1, q, s, few, 2 * few)).astype(BF16)
        stage_copy(b, q).start()
        for s in range(2):
            acc[q, s, :few * part] = acc[q, s, :few * part] + received(b - 1, q, s, 0, few)

    order = list(range(1, col_bits)) + [0]

    def chosen(done, bit, which):
        return tuple(0 if d in done else which if d == bit else slice(None) for d in range(col_bits))

    def spare_copy(j, u):
        return remote(s_sends[j].at[u], s_recvs[j].at[u], (s_sem.at[0, j, u], s_sem.at[1, j, u]),
                      {"col": flip(col_me, 1 << order[j])})

    def spare_multiply(u):
        c = chunks - spare + u
        for s in range(2):
            lhs = signed[groups - 1, s].reshape(cols * part, cd_width)
            total = jnp.dot(lhs, held[c, s], preferred_element_type=F32).reshape((2,) * col_bits + (part, chunk))
            s_acc[u, s] = total
            s_sends[0][u, s] = total[chosen((), order[0], 1)].astype(BF16)
        spare_copy(0, u).start()

    def spare_reduce(j, u):
        spare_copy(j - 1, u).wait()
        left = [d for d in range(col_bits) if d not in order[:j]]
        for s in range(2):
            kept = s_acc[(u, s) + chosen(order[:j], None, 0)] + s_recvs[j - 1][u, s].astype(F32)
            pick = lambda which: tuple(which if d == order[j] else slice(None) for d in left)
            s_sends[j][u, s] = kept[pick(1)].astype(BF16)
            s_acc[(u, s) + chosen(order[:j], order[j], 0)] = kept[pick(0)]
        spare_copy(j, u).start()

    def spare_combine(u):
        spare_copy(col_bits - 1, u).wait()
        kept = [s_acc[(u, s) + (0,) * col_bits] + s_recvs[-1][u, s].astype(F32) for s in range(2)]
        finish(ordinary + u, kept)

    def out_rows(q, l, which):
        g, c = q // chunks, q % chunks
        return pl.ds(g * (part * 2 * ab_tiles) + 2 * (c * lanes + l) + which, part, stride=2 * ab_tiles)

    def finish(q, kept):
        for l in range(lanes):
            plus, minus = (x[:, l * TILE:(l + 1) * TILE] for x in kept)
            at = pl.ds(l * TILE, TILE)
            index = jnp.broadcast_to(inverse[pl.ds(q % chunks * lanes + l, 1), :], (part, TILE))
            msend[q, :, at] = jnp.take_along_axis(0.5 * (plus - minus), index, axis=1)
            out[out_rows(q, l, 0), :] = 0.5 * (plus + minus)
        mirror_copy(q).start()

    def combine(q):
        stage_copy(col_bits - 1, q).wait()
        finish(q, [acc[q, s, :part] + recvs[-1][q, s].astype(F32) for s in range(2)])

    def place(q):
        mirror_copy(q).wait()
        for l in range(lanes):
            out[out_rows(q, l, 1), :] = mrecv[q, :, pl.ds(l * TILE, TILE)]

    a_copy().wait()
    stage_flip(0)
    pl.semaphore_wait(barrier, col_bits + row_bits)
    f_copy(0).start()
    for n in range(1, len(flips)):
        stage_flip(n)

    cut = lambda x: chunks * x // 8
    lax.fori_loop(0, ab_tiles, invert, 0, unroll=UNROLL)
    keep_range(0, cut(KEEPS[0]))
    make_signed(0)
    gather_first(0, 1)
    keep_range(cut(KEEPS[0]), cut(KEEPS[1]))
    gather_core(0, 1)
    lax.fori_loop(0, split, functools.partial(multiply_away, 0), 0)
    if row_bits > 1:
        gather_next(0, 0, 1)
    keep_range(cut(KEEPS[1]), cut(KEEPS[2]))
    make_signed(1)
    gather_first(0, 0)
    for stage in range(1, row_bits):
        gather_next(0, stage, 1)
    for a in range(1, classes):
        lax.fori_loop(0, split, functools.partial(multiply_away, a), 0)
    lax.fori_loop(split, early, multiply_leaving, 0)
    for stage in range(row_bits - 1):
        gather_next(0, stage, 0)
    keep_range(cut(KEEPS[2]), chunks)
    gather_core(0, 0)
    gather_next(0, row_bits - 1, 0)

    start = min(early, LAGS[0])
    events, after = [], []
    for g in range(1, groups):
        last = g * chunks
        for k in reversed(range(per_row)):
            begin = max(last - EVENTS[0] - EVENTS[1] * k, start)
            events.append((begin, functools.partial(make_signed, (g + 1) * per_row - 1 - k)))
            events.append((begin, functools.partial(gather_first, g, k)))
            for stage in range(row_bits - 1):
                events.append((min(begin + stage + 1, last), functools.partial(gather_next, g, stage, k)))
            events.append((last, functools.partial(gather_core, g, k)))
            events.append((last, functools.partial(gather_next, g, row_bits - 1, k)))
    for u in range(spare):
        begin = (groups - 1) * chunks + SPARE[1] + u
        late = [(begin, functools.partial(spare_multiply, u))]
        for j in range(1, col_bits):
            late.append((begin + SPARE[2] * j, functools.partial(spare_reduce, j, u)))
        late.append((begin + SPARE[2] * col_bits, functools.partial(spare_combine, u)))
        late.append((begin + SPARE[2] * col_bits + LAGS[2], functools.partial(place, ordinary + u)))
        after.extend(late)
    end = max([ordinary + LAGS[0] + (col_bits - 1) * LAGS[1] + LAGS[2]] + [w + 1 for w, _ in after])

    def act(i, listed):
        for when in sorted(set(w for w, _ in listed)):
            @pl.when(i == when)
            def _():
                for w, action in listed:
                    if w == when:
                        action()

    def step(i, carry):
        act(i, events)

        @pl.when((i >= early) & (i < ordinary))
        def _():
            multiply(i)

        @pl.when((i >= LAGS[0]) & (i < early + LAGS[0]))
        def _():
            multiply_own(i - LAGS[0], 0)

        lag = 0
        for b in range(1, col_bits):
            lag += LAGS[min(b - 1, 1)]

            @pl.when((i >= lag) & (i < ordinary + lag))
            def _():
                reduce(b, i - lag)

        lag += LAGS[1]

        @pl.when((i >= lag) & (i < ordinary + lag))
        def _():
            combine(i - lag)

        lag += LAGS[2]

        @pl.when((i >= lag) & (i < ordinary + lag))
        def _():
            place(i - lag)

        act(i, after)
        return carry

    lax.fori_loop(start, end, step, 0)
    for n in range(len(flips)):
        f_copy(n).wait_send()


def body(amplitudes, integrals, screen, mirror, denominators):
    cols, rows = lax.axis_size("col"), lax.axis_size("row")
    col_bits = cols.bit_length() - 1
    occ, _, cd_width = amplitudes.shape
    own, _, ab_width = denominators.shape
    per_row = occ // own
    groups = 2 if own % 32 == 0 else 1
    part = own // groups
    chunk = min(CHUNK, ab_width)
    chunks = ab_width // chunk
    pieces = groups * chunks
    tiles, ab_tiles = cd_width // TILE, ab_width // TILE
    early, split = min(EARLY[0], chunks), min(EARLY[1], chunks)
    spare = SPARE[0] if pieces >= 16 else 0
    flips = groups * per_row
    far = max(flips - NEAR, 1)
    vmem = pl.BlockSpec(memory_space=pltpu.VMEM)
    shape = lambda b: (pieces, 2, (cols >> b + 1) * part, chunk)
    pairs = amplitudes.reshape(occ, 2, tiles, TILE).transpose(0, 2, 1, 3).reshape(occ * tiles * 2, TILE)
    out = pl.pallas_call(
        functools.partial(kernel, (rows, cols, groups, per_row, part, tiles, ab_tiles, early, split, spare)),
        out_shape=jax.ShapeDtypeStruct((own * ab_tiles * 2, TILE), F32),
        in_specs=[pl.BlockSpec(memory_space=pl.ANY), vmem, pl.BlockSpec(memory_space=pltpu.SMEM),
                  pl.BlockSpec(memory_space=pl.ANY)],
        out_specs=vmem,
        scratch_shapes=[
            pltpu.VMEM((occ * tiles * 2, TILE), F32),
            pltpu.VMEM((chunks, 2, cd_width, chunk), BF16),
            pltpu.VMEM((NEAR, part, cd_width), BF16),
            pltpu.VMEM((NEAR, part, cd_width), BF16),
            pltpu.VMEM((far, part, cd_width), F32),
            pltpu.VMEM((far, part, cd_width), F32),
            pltpu.VMEM((groups, 2, per_row, 2, rows // 2, part, cd_width), BF16),
            pltpu.VMEM(shape(0), F32),
            pltpu.VMEM((ab_tiles, TILE), jnp.int32),
        ] + ([pltpu.VMEM((pieces, 2, 2, rows // 2, part, chunk), BF16)] + [pltpu.VMEM(shape(b), BF16) for b in range(1, col_bits)]) * 2 + [
            pltpu.VMEM((pieces, part, chunk), F32),
            pltpu.VMEM((pieces, part, chunk), F32),
            pltpu.SemaphoreType.DMA((1,)),
            pltpu.SemaphoreType.DMA((chunks, 2)),
            pltpu.SemaphoreType.DMA((2, flips)),
            pltpu.SemaphoreType.DMA((2, groups * rows * per_row)),
            pltpu.SemaphoreType.DMA((2, col_bits, pieces)),
            pltpu.SemaphoreType.DMA((2, pieces)),
        ] + ([
            pltpu.SemaphoreType.DMA((2, col_bits, spare)),
            pltpu.VMEM((spare, 2) + (2,) * col_bits + (part, chunk), F32),
        ] + [pltpu.VMEM((spare, 2) + (2,) * (col_bits - 1 - b) + (part, chunk), BF16) for b in range(col_bits)] * 2 if spare else []),
        compiler_params=pltpu.CompilerParams(
            collective_id=0, has_side_effects=True, vmem_limit_bytes=60 * 1024 * 1024),
    )(pairs, mirror.reshape(-1, TILE), screen, integrals)
    divisors = denominators.reshape(own, 2, ab_tiles, TILE).transpose(0, 2, 1, 3).reshape(own * ab_tiles * 2, TILE)
    update = out / divisors
    return update.reshape(own, ab_tiles, 2, TILE).transpose(0, 2, 1, 3).reshape(own, 2, ab_width)


def solution(mesh):
    in_specs = (
        P("row", None, "col"),
        P(None, "col", "row"),
        P(None, "col", "row"),
        P(),
        P("col", None, "row"),
    )
    out_specs = P("col", None, "row")
    return jax.shard_map(body, mesh=mesh, in_specs=in_specs, out_specs=out_specs, check_vma=False)
```

```python
import functools

import jax
import jax.numpy as jnp
from jax import lax
from jax.experimental import pallas as pl
from jax.experimental.pallas import tpu as pltpu
from jax.sharding import PartitionSpec as P

TILE = 128
CHUNK = 512
LAGS = (2, 3, 4)
NEAR = 2
FOLLOW = {}
KEEPS = (3, 4, 6)
EARLY = (4, 2)
UNROLL = 8
EVENTS = (1, 3)
SPARE = (1, 1, 4)
F32, BF16 = jnp.float32, jnp.bfloat16


def flip(x, bits):
    result = x
    place = 0
    while bits >> place:
        if bits >> place & 1:
            result = result + (1 - 2 * (x // (1 << place) % 2)) * (1 << place)
        place += 1
    return result


def position(owner, me, bits):
    total = 0
    for i in range(bits):
        differs = (owner // (1 << i) + me // (1 << i)) % 2
        total = total + differs * (1 << (bits - 1 - i))
    return total


def kernel(sizes, amps, mirror, screen, integrals, out,
           loaded, held, near_src, near_dst, flip_src, flip_dst, signed, acc, inverse, *rest):
    rows, cols, groups, per_row, part, tiles, ab_tiles, early, split, spare = sizes
    row_bits, col_bits = rows.bit_length() - 1, cols.bit_length() - 1
    sends, recvs = rest[:col_bits], rest[col_bits:2 * col_bits]
    rest = rest[2 * col_bits:]
    msend, mrecv, a_sem, k_sem, f_sem, g_sem, r_sem, m_sem = rest[:8]
    rest = rest[8:]
    if spare:
        s_sem, s_acc, s_sends, s_recvs = rest[0], rest[1], rest[2:2 + col_bits], rest[2 + col_bits:]
    cd_width = tiles * TILE
    chunk = held.shape[-1]
    lanes = chunk // TILE
    chunks = ab_tiles // lanes
    pieces = groups * chunks
    row_me, col_me = lax.axis_index("row"), lax.axis_index("col")
    half = cols * part // 2
    classes = rows // 2
    ordinary = pieces - spare

    def a_copy():
        return pltpu.make_async_copy(amps, loaded, a_sem.at[0])

    def k_copy(c, s):
        return pltpu.make_async_copy(
            integrals.at[s, :, pl.ds(pl.multiple_of(c * chunk, chunk), chunk)], held.at[c, s], k_sem.at[c, s])

    def start_k(c, carry):
        for s in range(2):
            k_copy(c, s).start()
        return carry

    a_copy().start()
    lax.fori_loop(0, chunks, start_k, 0)

    barrier = pltpu.get_barrier_semaphore()
    for b in range(col_bits):
        pl.semaphore_signal(barrier, inc=1, device_id={"col": flip(col_me, 1 << b)}, device_id_type=pl.DeviceIdType.MESH)
    for b in range(row_bits):
        pl.semaphore_signal(barrier, inc=1, device_id={"row": flip(row_me, 1 << b)}, device_id_type=pl.DeviceIdType.MESH)

    def remote(src, dst, sem, target):
        return pltpu.make_async_remote_copy(
            src_ref=src, dst_ref=dst, send_sem=sem[0], recv_sem=sem[1],
            device_id=target, device_id_type=pl.DeviceIdType.MESH)

    flips = [(g, k) for g in range(groups) for k in reversed(range(per_row))]

    def member(k):
        total = 0
        for i in range(per_row.bit_length() - 1):
            total = total + (k // (1 << i) % 2 + col_me // (1 << i)) % 2 * (1 << i)
        return total

    def amp_rows(g, k, t, which):
        first = (member(k) * groups + g) * part
        return loaded[pl.ds(first * (2 * tiles) + 2 * t + which, part, stride=2 * tiles), :]

    def f_copy(n):
        src, dst = (near_src.at[n], near_dst.at[n]) if n < NEAR else (flip_src.at[n - NEAR], flip_dst.at[n - NEAR])
        return remote(src, dst, (f_sem.at[0, n], f_sem.at[1, n]), {"col": flip(col_me, cols // 2)})

    def stage_flip(n):
        g, k = flips[n]
        for t in range(tiles):
            at = pl.ds(t * TILE, TILE)
            value = amp_rows(g, k, t, 1)
            if n < NEAR:
                near_src[n, :, at] = value.astype(BF16)
            else:
                flip_src[n - NEAR, :, at] = value

    def place_of(shard):
        return position(shard, col_me // per_row, row_bits)

    def gather_copy(g, stage, k, t):
        bit = row_bits - 1 - stage
        pos = place_of(flip(row_me, t << (bit + 1)))
        i = (g * rows + (1 << stage) - 1 + t) * per_row + k
        block = signed.at[g, :, k, pos // classes, pos % classes]
        return remote(block, block, (g_sem.at[0, i], g_sem.at[1, i]), {"row": flip(row_me, 1 << bit)})

    def gather_first(g, k):
        for stage in range(row_bits):
            gather_copy(g, stage, k, 0).start()

    def gather_core(g, k):
        gather_copy(g, row_bits - 1, k, 0).wait()

    def gather_next(g, stage, k):
        final = stage == row_bits - 1
        for t in range(1 if final else 0, 1 << stage):
            gather_copy(g, stage, k, t).wait()
        if not final:
            for t in range(1, 2 << stage):
                gather_copy(g, stage + 1, k, t).start()

    def make_signed(n):
        g, k = flips[n]
        f_copy(n).wait_recv()
        for later in FOLLOW.get(n, (n + 1,)):
            if later < len(flips):
                f_copy(later).start()
        pos = place_of(row_me)
        for t in range(tiles):
            at = pl.ds(t * TILE, TILE)
            index = jnp.broadcast_to(mirror[pl.ds(col_me * tiles + t, 1), :] % TILE, (part, TILE))
            arrived = near_dst[n, :, at].astype(F32) if n < NEAR else flip_dst[n - NEAR, :, at]
            flipped = jnp.take_along_axis(arrived, index, axis=1)
            mine = amp_rows(g, k, t, 0)
            signed[g, 0, k, pos // classes, pos % classes, :, at] = (mine + flipped).astype(BF16)
            signed[g, 1, k, pos // classes, pos % classes, :, at] = (mine - flipped).astype(BF16)

    def keep_tiles(c):
        for s in range(2):
            k_copy(c, s).wait()

            def one(t, carry):
                for l in range(lanes):
                    factor = jnp.full((16, TILE), screen[s, t, c * lanes + l]).astype(F32).astype(BF16)
                    at = (c, s, pl.ds(pl.multiple_of(t * TILE, TILE), TILE), pl.ds(l * TILE, TILE))
                    block = held[at].reshape(TILE // 16, 16, TILE)
                    held[at] = (block * factor[None]).reshape(TILE, TILE)
                return carry

            lax.fori_loop(0, tiles, one, 0, unroll=2)

    def keep_range(lo, hi):
        def one(c, carry):
            keep_tiles(c)
            return carry

        if hi > lo:
            lax.fori_loop(lo, hi, one, 0)

    def invert(t, carry):
        index = jnp.broadcast_to(mirror[pl.ds(row_me * ab_tiles + t, 1), :] % TILE, (TILE, TILE))
        hit = jnp.where(lax.broadcasted_iota(jnp.int32, (TILE, TILE), 0) == index, 1.0, 0.0).astype(BF16)
        places = lax.broadcasted_iota(jnp.int32, (16, TILE), 1).astype(F32).astype(BF16)
        found = lax.dot_general(places, hit, (((1,), (1,)), ((), ())), preferred_element_type=F32)
        inverse[pl.ds(t, 1), :] = found[:1].astype(jnp.int32)
        return carry

    def stage_copy(b, q):
        return remote(sends[b].at[q], recvs[b].at[q], (r_sem.at[0, b, q], r_sem.at[1, b, q]),
                      {"col": flip(col_me, 1 << b)})

    def mirror_copy(q):
        return remote(msend.at[q], mrecv.at[q], (m_sem.at[0, q], m_sem.at[1, q]),
                      {"row": flip(row_me, rows // 2)})

    def early_copy(q, a):
        return remote(sends[0].at[q, :, :, a], recvs[0].at[q, :, :, a], (r_sem.at[0, 0, q], r_sem.at[1, 0, q]),
                      {"col": flip(col_me, 1)})

    def multiply_away(j, q, carry):
        a = flip(place_of(row_me) % classes, j)
        for s in range(2):
            lhs = signed[0, s, per_row - 1, :, a].reshape(2 * part, cd_width)
            total = jnp.dot(lhs, held[q, s], preferred_element_type=F32).astype(BF16)
            sends[0][q, s, :, a] = total.reshape(2, part, chunk)
        early_copy(q, a).start()
        return carry

    def multiply_leaving(q, carry):
        for s in range(2):
            lhs = signed[0, s, per_row - 1].reshape(half, cd_width)
            total = jnp.dot(lhs, held[q, s], preferred_element_type=F32).astype(BF16)
            sends[0][q, s] = total.reshape(2, classes, part, chunk)
        stage_copy(0, q).start()
        return carry

    def multiply_own(q, carry):
        for s in range(2):
            lhs = signed[0, s, 0].reshape(half, cd_width)
            acc[q, s] = jnp.dot(lhs, held[q, s], preferred_element_type=F32)
        return carry

    def multiply(q):
        g, c = q // chunks, q % chunks
        for s in range(2):
            lhs = signed[g, s].reshape(cols * part, cd_width)
            total = jnp.dot(lhs, held[c, s], preferred_element_type=F32)
            sends[0][q, s] = total[half:].astype(BF16).reshape(2, classes, part, chunk)
            acc[q, s] = total[:half]
        stage_copy(0, q).start()

    def received(b, q, s, lo, hi):
        if b:
            return recvs[b][q, s, lo * part:hi * part].astype(F32)
        lo, hi = lo // classes, max(hi // classes, 1)
        return recvs[b][q, s, lo:hi].reshape((hi - lo) * classes * part, chunk).astype(F32)

    def reduce(b, q):
        stage_copy(b - 1, q).wait()
        few = (cols >> b) // 2
        for s in range(2):
            sends[b][q, s] = (acc[q, s, few * part:2 * few * part] + received(b - 1, q, s, few, 2 * few)).astype(BF16)
        stage_copy(b, q).start()
        for s in range(2):
            acc[q, s, :few * part] = acc[q, s, :few * part] + received(b - 1, q, s, 0, few)

    order = list(range(1, col_bits)) + [0]

    def chosen(done, bit, which):
        return tuple(0 if d in done else which if d == bit else slice(None) for d in range(col_bits))

    def spare_copy(j, u):
        return remote(s_sends[j].at[u], s_recvs[j].at[u], (s_sem.at[0, j, u], s_sem.at[1, j, u]),
                      {"col": flip(col_me, 1 << order[j])})

    def spare_multiply(u):
        c = chunks - spare + u
        for s in range(2):
            lhs = signed[groups - 1, s].reshape(cols * part, cd_width)
            total = jnp.dot(lhs, held[c, s], preferred_element_type=F32).reshape((2,) * col_bits + (part, chunk))
            s_acc[u, s] = total
            s_sends[0][u, s] = total[chosen((), order[0], 1)].astype(BF16)
        spare_copy(0, u).start()

    def spare_reduce(j, u):
        spare_copy(j - 1, u).wait()
        left = [d for d in range(col_bits) if d not in order[:j]]
        for s in range(2):
            kept = s_acc[(u, s) + chosen(order[:j], None, 0)] + s_recvs[j - 1][u, s].astype(F32)
            pick = lambda which: tuple(which if d == order[j] else slice(None) for d in left)
            s_sends[j][u, s] = kept[pick(1)].astype(BF16)
            s_acc[(u, s) + chosen(order[:j], order[j], 0)] = kept[pick(0)]
        spare_copy(j, u).start()

    def spare_combine(u):
        spare_copy(col_bits - 1, u).wait()
        kept = [s_acc[(u, s) + (0,) * col_bits] + s_recvs[-1][u, s].astype(F32) for s in range(2)]
        finish(ordinary + u, kept)

    def out_rows(q, l, which):
        g, c = q // chunks, q % chunks
        return pl.ds(g * (part * 2 * ab_tiles) + 2 * (c * lanes + l) + which, part, stride=2 * ab_tiles)

    def finish(q, kept):
        for l in range(lanes):
            plus, minus = (x[:, l * TILE:(l + 1) * TILE] for x in kept)
            at = pl.ds(l * TILE, TILE)
            index = jnp.broadcast_to(inverse[pl.ds(q % chunks * lanes + l, 1), :], (part, TILE))
            msend[q, :, at] = jnp.take_along_axis(0.5 * (plus - minus), index, axis=1)
            out[out_rows(q, l, 0), :] = 0.5 * (plus + minus)
        mirror_copy(q).start()

    def combine(q):
        stage_copy(col_bits - 1, q).wait()
        finish(q, [acc[q, s, :part] + recvs[-1][q, s].astype(F32) for s in range(2)])

    def place(q):
        mirror_copy(q).wait()
        for l in range(lanes):
            out[out_rows(q, l, 1), :] = mrecv[q, :, pl.ds(l * TILE, TILE)]

    a_copy().wait()
    stage_flip(0)
    pl.semaphore_wait(barrier, col_bits + row_bits)
    f_copy(0).start()
    for n in range(1, len(flips)):
        stage_flip(n)

    cut = lambda x: chunks * x // 8
    lax.fori_loop(0, ab_tiles, invert, 0, unroll=UNROLL)
    keep_range(0, cut(KEEPS[0]))
    make_signed(0)
    gather_first(0, 1)
    keep_range(cut(KEEPS[0]), cut(KEEPS[1]))
    gather_core(0, 1)
    lax.fori_loop(0, split, functools.partial(multiply_away, 0), 0)
    if row_bits > 1:
        gather_next(0, 0, 1)
    keep_range(cut(KEEPS[1]), cut(KEEPS[2]))
    make_signed(1)
    gather_first(0, 0)
    for stage in range(1, row_bits):
        gather_next(0, stage, 1)
    for a in range(1, classes):
        lax.fori_loop(0, split, functools.partial(multiply_away, a), 0)
    lax.fori_loop(split, early, multiply_leaving, 0)
    for stage in range(row_bits - 1):
        gather_next(0, stage, 0)
    keep_range(cut(KEEPS[2]), chunks)
    gather_core(0, 0)
    gather_next(0, row_bits - 1, 0)

    start = min(early, LAGS[0])
    events, after = [], []
    for g in range(1, groups):
        last = g * chunks
        for k in reversed(range(per_row)):
            begin = max(last - EVENTS[0] - EVENTS[1] * k, start)
            events.append((begin, functools.partial(make_signed, (g + 1) * per_row - 1 - k)))
            events.append((begin, functools.partial(gather_first, g, k)))
            for stage in range(row_bits - 1):
                events.append((min(begin + stage + 1, last), functools.partial(gather_next, g, stage, k)))
            events.append((last, functools.partial(gather_core, g, k)))
            events.append((last, functools.partial(gather_next, g, row_bits - 1, k)))
    for u in range(spare):
        begin = (groups - 1) * chunks + SPARE[1] + u
        late = [(begin, functools.partial(spare_multiply, u))]
        for j in range(1, col_bits):
            late.append((begin + SPARE[2] * j, functools.partial(spare_reduce, j, u)))
        late.append((begin + SPARE[2] * col_bits, functools.partial(spare_combine, u)))
        late.append((begin + SPARE[2] * col_bits + LAGS[2], functools.partial(place, ordinary + u)))
        after.extend(late)
    end = max([ordinary + LAGS[0] + (col_bits - 1) * LAGS[1] + LAGS[2]] + [w + 1 for w, _ in after])

    def act(i, listed):
        for when in sorted(set(w for w, _ in listed)):
            @pl.when(i == when)
            def _():
                for w, action in listed:
                    if w == when:
                        action()

    def step(i, carry):
        act(i, events)

        @pl.when((i >= early) & (i < ordinary))
        def _():
            multiply(i)

        def late(lag, action):
            @pl.when((i >= lag) & (i < ordinary + lag))
            def _():
                action(i - lag)

        for b in reversed(range(2, col_bits)):
            late(LAGS[0] + (b - 1) * LAGS[1], functools.partial(reduce, b))
        late(LAGS[0] + (col_bits - 1) * LAGS[1], combine)
        late(LAGS[0] + (col_bits - 1) * LAGS[1] + LAGS[2], place)

        @pl.when((i >= LAGS[0]) & (i < early + LAGS[0]))
        def _():
            multiply_own(i - LAGS[0], 0)

        late(LAGS[0], functools.partial(reduce, 1))
        act(i, after)
        return carry

    lax.fori_loop(start, end, step, 0)
    for n in range(len(flips)):
        f_copy(n).wait_send()


def body(amplitudes, integrals, screen, mirror, denominators):
    cols, rows = lax.axis_size("col"), lax.axis_size("row")
    col_bits = cols.bit_length() - 1
    occ, _, cd_width = amplitudes.shape
    own, _, ab_width = denominators.shape
    per_row = occ // own
    groups = 2 if own % 32 == 0 else 1
    part = own // groups
    chunk = min(CHUNK, ab_width)
    chunks = ab_width // chunk
    pieces = groups * chunks
    tiles, ab_tiles = cd_width // TILE, ab_width // TILE
    early, split = min(EARLY[0], chunks), min(EARLY[1], chunks)
    spare = SPARE[0] if pieces >= 16 else 0
    flips = groups * per_row
    far = max(flips - NEAR, 1)
    vmem = pl.BlockSpec(memory_space=pltpu.VMEM)
    shape = lambda b: (pieces, 2, (cols >> b + 1) * part, chunk)
    pairs = amplitudes.reshape(occ, 2, tiles, TILE).transpose(0, 2, 1, 3).reshape(occ * tiles * 2, TILE)
    out = pl.pallas_call(
        functools.partial(kernel, (rows, cols, groups, per_row, part, tiles, ab_tiles, early, split, spare)),
        out_shape=jax.ShapeDtypeStruct((own * ab_tiles * 2, TILE), F32),
        in_specs=[pl.BlockSpec(memory_space=pl.ANY), vmem, pl.BlockSpec(memory_space=pltpu.SMEM),
                  pl.BlockSpec(memory_space=pl.ANY)],
        out_specs=vmem,
        scratch_shapes=[
            pltpu.VMEM((occ * tiles * 2, TILE), F32),
            pltpu.VMEM((chunks, 2, cd_width, chunk), BF16),
            pltpu.VMEM((NEAR, part, cd_width), BF16),
            pltpu.VMEM((NEAR, part, cd_width), BF16),
            pltpu.VMEM((far, part, cd_width), F32),
            pltpu.VMEM((far, part, cd_width), F32),
            pltpu.VMEM((groups, 2, per_row, 2, rows // 2, part, cd_width), BF16),
            pltpu.VMEM(shape(0), F32),
            pltpu.VMEM((ab_tiles, TILE), jnp.int32),
        ] + ([pltpu.VMEM((pieces, 2, 2, rows // 2, part, chunk), BF16)] + [pltpu.VMEM(shape(b), BF16) for b in range(1, col_bits)]) * 2 + [
            pltpu.VMEM((pieces, part, chunk), F32),
            pltpu.VMEM((pieces, part, chunk), F32),
            pltpu.SemaphoreType.DMA((1,)),
            pltpu.SemaphoreType.DMA((chunks, 2)),
            pltpu.SemaphoreType.DMA((2, flips)),
            pltpu.SemaphoreType.DMA((2, groups * rows * per_row)),
            pltpu.SemaphoreType.DMA((2, col_bits, pieces)),
            pltpu.SemaphoreType.DMA((2, pieces)),
        ] + ([
            pltpu.SemaphoreType.DMA((2, col_bits, spare)),
            pltpu.VMEM((spare, 2) + (2,) * col_bits + (part, chunk), F32),
        ] + [pltpu.VMEM((spare, 2) + (2,) * (col_bits - 1 - b) + (part, chunk), BF16) for b in range(col_bits)] * 2 if spare else []),
        compiler_params=pltpu.CompilerParams(
            collective_id=0, has_side_effects=True, vmem_limit_bytes=60 * 1024 * 1024),
    )(pairs, mirror.reshape(-1, TILE), screen, integrals)
    divisors = denominators.reshape(own, 2, ab_tiles, TILE).transpose(0, 2, 1, 3).reshape(own * ab_tiles * 2, TILE)
    update = out / divisors
    return update.reshape(own, ab_tiles, 2, TILE).transpose(0, 2, 1, 3).reshape(own, 2, ab_width)


def solution(mesh):
    in_specs = (
        P("row", None, "col"),
        P(None, "col", "row"),
        P(None, "col", "row"),
        P(),
        P("col", None, "row"),
    )
    out_specs = P("col", None, "row")
    return jax.shard_map(body, mesh=mesh, in_specs=in_specs, out_specs=out_specs, check_vma=False)
```

```python
import functools

import jax
import jax.numpy as jnp
from jax import lax
from jax.experimental import pallas as pl
from jax.experimental.pallas import tpu as pltpu
from jax.sharding import PartitionSpec as P

TILE = 128
CHUNK = 512
LAGS = (2, 3, 4)
NEAR = 2
FOLLOW = {}
KEEPS = (3, 4, 6)
EARLY = (4, 2)
UNROLL = 8
EVENTS = (1, 3)
SPARE = (1, 1, 4)
F32, BF16 = jnp.float32, jnp.bfloat16


def flip(x, bits):
    result = x
    place = 0
    while bits >> place:
        if bits >> place & 1:
            result = result + (1 - 2 * (x // (1 << place) % 2)) * (1 << place)
        place += 1
    return result


def position(owner, me, bits):
    total = 0
    for i in range(bits):
        differs = (owner // (1 << i) + me // (1 << i)) % 2
        total = total + differs * (1 << (bits - 1 - i))
    return total


def kernel(sizes, amps, mirror, screen, integrals, written, out,
           loaded, held, near_src, near_dst, flip_src, flip_dst, signed, acc, inverse, *rest):
    rows, cols, groups, per_row, part, tiles, ab_tiles, early, split, spare = sizes
    row_bits, col_bits = rows.bit_length() - 1, cols.bit_length() - 1
    sends, recvs = rest[:col_bits], rest[col_bits:2 * col_bits]
    rest = rest[2 * col_bits:]
    msend, mrecv, a_sem, k_sem, f_sem, g_sem, r_sem, m_sem, o_sem = rest[:9]
    rest = rest[9:]
    if spare:
        s_sem, s_acc, s_sends, s_recvs = rest[0], rest[1], rest[2:2 + col_bits], rest[2 + col_bits:]
    cd_width = tiles * TILE
    chunk = held.shape[-1]
    lanes = chunk // TILE
    chunks = ab_tiles // lanes
    pieces = groups * chunks
    row_me, col_me = lax.axis_index("row"), lax.axis_index("col")
    half = cols * part // 2
    classes = rows // 2
    ordinary = pieces - spare

    def a_copy():
        return pltpu.make_async_copy(amps, loaded.at[pl.ds(0, amps.shape[0])], a_sem.at[0])

    def o_copy(g):
        at = pl.ds(g * (part * 2 * ab_tiles), part * 2 * ab_tiles)
        return pltpu.make_async_copy(out.at[at], written.at[at], o_sem.at[g])

    def k_copy(c, s):
        return pltpu.make_async_copy(
            integrals.at[s, :, pl.ds(pl.multiple_of(c * chunk, chunk), chunk)], held.at[c, s], k_sem.at[c, s])

    def start_k(c, carry):
        for s in range(2):
            k_copy(c, s).start()
        return carry

    a_copy().start()
    lax.fori_loop(0, chunks, start_k, 0)

    barrier = pltpu.get_barrier_semaphore()
    for b in range(col_bits):
        pl.semaphore_signal(barrier, inc=1, device_id={"col": flip(col_me, 1 << b)}, device_id_type=pl.DeviceIdType.MESH)
    for b in range(row_bits):
        pl.semaphore_signal(barrier, inc=1, device_id={"row": flip(row_me, 1 << b)}, device_id_type=pl.DeviceIdType.MESH)

    def remote(src, dst, sem, target):
        return pltpu.make_async_remote_copy(
            src_ref=src, dst_ref=dst, send_sem=sem[0], recv_sem=sem[1],
            device_id=target, device_id_type=pl.DeviceIdType.MESH)

    flips = [(g, k) for g in range(groups) for k in reversed(range(per_row))]

    def member(k):
        total = 0
        for i in range(per_row.bit_length() - 1):
            total = total + (k // (1 << i) % 2 + col_me // (1 << i)) % 2 * (1 << i)
        return total

    def amp_rows(g, k, t, which):
        first = (member(k) * groups + g) * part
        return loaded[pl.ds(first * (2 * tiles) + 2 * t + which, part, stride=2 * tiles), :]

    def f_copy(n):
        src, dst = (near_src.at[n], near_dst.at[n]) if n < NEAR else (flip_src.at[n - NEAR], flip_dst.at[n - NEAR])
        return remote(src, dst, (f_sem.at[0, n], f_sem.at[1, n]), {"col": flip(col_me, cols // 2)})

    def stage_flip(n):
        g, k = flips[n]
        for t in range(tiles):
            at = pl.ds(t * TILE, TILE)
            value = amp_rows(g, k, t, 1)
            if n < NEAR:
                near_src[n, :, at] = value.astype(BF16)
            else:
                flip_src[n - NEAR, :, at] = value

    def place_of(shard):
        return position(shard, col_me // per_row, row_bits)

    def gather_copy(g, stage, k, t):
        bit = row_bits - 1 - stage
        pos = place_of(flip(row_me, t << (bit + 1)))
        i = (g * rows + (1 << stage) - 1 + t) * per_row + k
        block = signed.at[g, :, k, pos // classes, pos % classes]
        return remote(block, block, (g_sem.at[0, i], g_sem.at[1, i]), {"row": flip(row_me, 1 << bit)})

    def gather_first(g, k):
        for stage in range(row_bits):
            gather_copy(g, stage, k, 0).start()

    def gather_core(g, k):
        gather_copy(g, row_bits - 1, k, 0).wait()

    def gather_next(g, stage, k):
        final = stage == row_bits - 1
        for t in range(1 if final else 0, 1 << stage):
            gather_copy(g, stage, k, t).wait()
        if not final:
            for t in range(1, 2 << stage):
                gather_copy(g, stage + 1, k, t).start()

    def make_signed(n):
        g, k = flips[n]
        f_copy(n).wait_recv()
        for later in FOLLOW.get(n, (n + 1,)):
            if later < len(flips):
                f_copy(later).start()
        pos = place_of(row_me)
        for t in range(tiles):
            at = pl.ds(t * TILE, TILE)
            index = jnp.broadcast_to(mirror[pl.ds(col_me * tiles + t, 1), :] % TILE, (part, TILE))
            arrived = near_dst[n, :, at].astype(F32) if n < NEAR else flip_dst[n - NEAR, :, at]
            flipped = jnp.take_along_axis(arrived, index, axis=1)
            mine = amp_rows(g, k, t, 0)
            signed[g, 0, k, pos // classes, pos % classes, :, at] = (mine + flipped).astype(BF16)
            signed[g, 1, k, pos // classes, pos % classes, :, at] = (mine - flipped).astype(BF16)

    def keep_tiles(c):
        for s in range(2):
            k_copy(c, s).wait()

            def one(t, carry):
                for l in range(lanes):
                    factor = jnp.full((16, TILE), screen[s, t, c * lanes + l]).astype(F32).astype(BF16)
                    at = (c, s, pl.ds(pl.multiple_of(t * TILE, TILE), TILE), pl.ds(l * TILE, TILE))
                    block = held[at].reshape(TILE // 16, 16, TILE)
                    held[at] = (block * factor[None]).reshape(TILE, TILE)
                return carry

            lax.fori_loop(0, tiles, one, 0, unroll=2)

    def keep_range(lo, hi):
        def one(c, carry):
            keep_tiles(c)
            return carry

        if hi > lo:
            lax.fori_loop(lo, hi, one, 0)

    def invert(t, carry):
        index = jnp.broadcast_to(mirror[pl.ds(row_me * ab_tiles + t, 1), :] % TILE, (TILE, TILE))
        hit = jnp.where(lax.broadcasted_iota(jnp.int32, (TILE, TILE), 0) == index, 1.0, 0.0).astype(BF16)
        places = lax.broadcasted_iota(jnp.int32, (16, TILE), 1).astype(F32).astype(BF16)
        found = lax.dot_general(places, hit, (((1,), (1,)), ((), ())), preferred_element_type=F32)
        inverse[pl.ds(t, 1), :] = found[:1].astype(jnp.int32)
        return carry

    def stage_copy(b, q):
        return remote(sends[b].at[q], recvs[b].at[q], (r_sem.at[0, b, q], r_sem.at[1, b, q]),
                      {"col": flip(col_me, 1 << b)})

    def mirror_copy(q):
        return remote(msend.at[q], mrecv.at[q], (m_sem.at[0, q], m_sem.at[1, q]),
                      {"row": flip(row_me, rows // 2)})

    def early_copy(q, a):
        return remote(sends[0].at[q, :, :, a], recvs[0].at[q, :, :, a], (r_sem.at[0, 0, q], r_sem.at[1, 0, q]),
                      {"col": flip(col_me, 1)})

    def multiply_away(j, q, carry):
        a = flip(place_of(row_me) % classes, j)
        for s in range(2):
            lhs = signed[0, s, per_row - 1, :, a].reshape(2 * part, cd_width)
            total = jnp.dot(lhs, held[q, s], preferred_element_type=F32).astype(BF16)
            sends[0][q, s, :, a] = total.reshape(2, part, chunk)
        early_copy(q, a).start()
        return carry

    def multiply_leaving(q, carry):
        for s in range(2):
            lhs = signed[0, s, per_row - 1].reshape(half, cd_width)
            total = jnp.dot(lhs, held[q, s], preferred_element_type=F32).astype(BF16)
            sends[0][q, s] = total.reshape(2, classes, part, chunk)
        stage_copy(0, q).start()
        return carry

    def multiply_own(q, carry):
        for s in range(2):
            lhs = signed[0, s, 0].reshape(half, cd_width)
            acc[q, s] = jnp.dot(lhs, held[q, s], preferred_element_type=F32)
        return carry

    def multiply(q):
        g, c = q // chunks, q % chunks
        for s in range(2):
            lhs = signed[g, s].reshape(cols * part, cd_width)
            total = jnp.dot(lhs, held[c, s], preferred_element_type=F32)
            sends[0][q, s] = total[half:].astype(BF16).reshape(2, classes, part, chunk)
            acc[q, s] = total[:half]
        stage_copy(0, q).start()

    def received(b, q, s, lo, hi):
        if b:
            return recvs[b][q, s, lo * part:hi * part].astype(F32)
        lo, hi = lo // classes, max(hi // classes, 1)
        return recvs[b][q, s, lo:hi].reshape((hi - lo) * classes * part, chunk).astype(F32)

    def reduce(b, q):
        stage_copy(b - 1, q).wait()
        few = (cols >> b) // 2
        for s in range(2):
            sends[b][q, s] = (acc[q, s, few * part:2 * few * part] + received(b - 1, q, s, few, 2 * few)).astype(BF16)
        stage_copy(b, q).start()
        for s in range(2):
            acc[q, s, :few * part] = acc[q, s, :few * part] + received(b - 1, q, s, 0, few)

    order = list(range(1, col_bits)) + [0]

    def chosen(done, bit, which):
        return tuple(0 if d in done else which if d == bit else slice(None) for d in range(col_bits))

    def spare_copy(j, u):
        return remote(s_sends[j].at[u], s_recvs[j].at[u], (s_sem.at[0, j, u], s_sem.at[1, j, u]),
                      {"col": flip(col_me, 1 << order[j])})

    def spare_multiply(u):
        c = chunks - spare + u
        for s in range(2):
            lhs = signed[groups - 1, s].reshape(cols * part, cd_width)
            total = jnp.dot(lhs, held[c, s], preferred_element_type=F32).reshape((2,) * col_bits + (part, chunk))
            s_acc[u, s] = total
            s_sends[0][u, s] = total[chosen((), order[0], 1)].astype(BF16)
        spare_copy(0, u).start()

    def spare_reduce(j, u):
        spare_copy(j - 1, u).wait()
        left = [d for d in range(col_bits) if d not in order[:j]]
        for s in range(2):
            kept = s_acc[(u, s) + chosen(order[:j], None, 0)] + s_recvs[j - 1][u, s].astype(F32)
            pick = lambda which: tuple(which if d == order[j] else slice(None) for d in left)
            s_sends[j][u, s] = kept[pick(1)].astype(BF16)
            s_acc[(u, s) + chosen(order[:j], order[j], 0)] = kept[pick(0)]
        spare_copy(j, u).start()

    def spare_combine(u):
        spare_copy(col_bits - 1, u).wait()
        kept = [s_acc[(u, s) + (0,) * col_bits] + s_recvs[-1][u, s].astype(F32) for s in range(2)]
        finish(ordinary + u, kept)

    def out_rows(q, l, which):
        g, c = q // chunks, q % chunks
        return pl.ds(g * (part * 2 * ab_tiles) + 2 * (c * lanes + l) + which, part, stride=2 * ab_tiles)

    def finish(q, kept):
        for l in range(lanes):
            plus, minus = (x[:, l * TILE:(l + 1) * TILE] for x in kept)
            at = pl.ds(l * TILE, TILE)
            index = jnp.broadcast_to(inverse[pl.ds(q % chunks * lanes + l, 1), :], (part, TILE))
            msend[q, :, at] = jnp.take_along_axis(0.5 * (plus - minus), index, axis=1)
            out[out_rows(q, l, 0), :] = 0.5 * (plus + minus)
        mirror_copy(q).start()

    def combine(q):
        stage_copy(col_bits - 1, q).wait()
        finish(q, [acc[q, s, :part] + recvs[-1][q, s].astype(F32) for s in range(2)])

    def place(q):
        mirror_copy(q).wait()
        for l in range(lanes):
            out[out_rows(q, l, 1), :] = mrecv[q, :, pl.ds(l * TILE, TILE)]

    a_copy().wait()
    stage_flip(0)
    pl.semaphore_wait(barrier, col_bits + row_bits)
    f_copy(0).start()
    for n in range(1, len(flips)):
        stage_flip(n)

    cut = lambda x: chunks * x // 8
    lax.fori_loop(0, ab_tiles, invert, 0, unroll=UNROLL)
    keep_range(0, cut(KEEPS[0]))
    make_signed(0)
    gather_first(0, 1)
    keep_range(cut(KEEPS[0]), cut(KEEPS[1]))
    gather_core(0, 1)
    lax.fori_loop(0, split, functools.partial(multiply_away, 0), 0)
    if row_bits > 1:
        gather_next(0, 0, 1)
    keep_range(cut(KEEPS[1]), cut(KEEPS[2]))
    make_signed(1)
    gather_first(0, 0)
    for stage in range(1, row_bits):
        gather_next(0, stage, 1)
    for a in range(1, classes):
        lax.fori_loop(0, split, functools.partial(multiply_away, a), 0)
    lax.fori_loop(split, early, multiply_leaving, 0)
    for stage in range(row_bits - 1):
        gather_next(0, stage, 0)
    keep_range(cut(KEEPS[2]), chunks)
    gather_core(0, 0)
    gather_next(0, row_bits - 1, 0)

    start = min(early, LAGS[0])
    events, after = [], []
    for g in range(1, groups):
        last = g * chunks
        for k in reversed(range(per_row)):
            begin = max(last - EVENTS[0] - EVENTS[1] * k, start)
            events.append((begin, functools.partial(make_signed, (g + 1) * per_row - 1 - k)))
            events.append((begin, functools.partial(gather_first, g, k)))
            for stage in range(row_bits - 1):
                events.append((min(begin + stage + 1, last), functools.partial(gather_next, g, stage, k)))
            events.append((last, functools.partial(gather_core, g, k)))
            events.append((last, functools.partial(gather_next, g, row_bits - 1, k)))
    for u in range(spare):
        begin = (groups - 1) * chunks + SPARE[1] + u
        late = [(begin, functools.partial(spare_multiply, u))]
        for j in range(1, col_bits):
            late.append((begin + SPARE[2] * j, functools.partial(spare_reduce, j, u)))
        late.append((begin + SPARE[2] * col_bits, functools.partial(spare_combine, u)))
        late.append((begin + SPARE[2] * col_bits + LAGS[2], functools.partial(place, ordinary + u)))
        after.extend(late)
    for g in range(groups - 1):
        done = (g + 1) * chunks - 1 + LAGS[0] + (col_bits - 1) * LAGS[1] + LAGS[2]
        after.append((done, functools.partial(lambda g: o_copy(g).start(), g)))
    end = max([ordinary + LAGS[0] + (col_bits - 1) * LAGS[1] + LAGS[2]] + [w + 1 for w, _ in after])

    def act(i, listed):
        for when in sorted(set(w for w, _ in listed)):
            @pl.when(i == when)
            def _():
                for w, action in listed:
                    if w == when:
                        action()

    def step(i, carry):
        act(i, events)

        @pl.when((i >= early) & (i < ordinary))
        def _():
            multiply(i)

        def late(lag, action):
            @pl.when((i >= lag) & (i < ordinary + lag))
            def _():
                action(i - lag)

        for b in reversed(range(2, col_bits)):
            late(LAGS[0] + (b - 1) * LAGS[1], functools.partial(reduce, b))
        late(LAGS[0] + (col_bits - 1) * LAGS[1], combine)
        late(LAGS[0] + (col_bits - 1) * LAGS[1] + LAGS[2], place)

        @pl.when((i >= LAGS[0]) & (i < early + LAGS[0]))
        def _():
            multiply_own(i - LAGS[0], 0)

        late(LAGS[0], functools.partial(reduce, 1))
        act(i, after)
        return carry

    lax.fori_loop(start, end, step, 0)
    o_copy(groups - 1).start()
    for g in range(groups):
        o_copy(g).wait()
    for n in range(len(flips)):
        f_copy(n).wait_send()


def body(amplitudes, integrals, screen, mirror, denominators):
    cols, rows = lax.axis_size("col"), lax.axis_size("row")
    col_bits = cols.bit_length() - 1
    occ, _, cd_width = amplitudes.shape
    own, _, ab_width = denominators.shape
    per_row = occ // own
    groups = 2 if own % 32 == 0 else 1
    part = own // groups
    chunk = min(CHUNK, ab_width)
    chunks = ab_width // chunk
    pieces = groups * chunks
    tiles, ab_tiles = cd_width // TILE, ab_width // TILE
    early, split = min(EARLY[0], chunks), min(EARLY[1], chunks)
    spare = SPARE[0] if pieces >= 16 else 0
    flips = groups * per_row
    far = max(flips - NEAR, 1)
    vmem = pl.BlockSpec(memory_space=pltpu.VMEM)
    shape = lambda b: (pieces, 2, (cols >> b + 1) * part, chunk)
    pairs = amplitudes.reshape(occ, 2, tiles, TILE).transpose(0, 2, 1, 3).reshape(occ * tiles * 2, TILE)
    out = pl.pallas_call(
        functools.partial(kernel, (rows, cols, groups, per_row, part, tiles, ab_tiles, early, split, spare)),
        out_shape=jax.ShapeDtypeStruct((own * ab_tiles * 2, TILE), F32),
        in_specs=[pl.BlockSpec(memory_space=pl.ANY), vmem, pl.BlockSpec(memory_space=pltpu.SMEM),
                  pl.BlockSpec(memory_space=pl.ANY)],
        out_specs=pl.BlockSpec(memory_space=pl.ANY),
        scratch_shapes=[
            pltpu.VMEM(((own + 1) * ab_tiles * 2, TILE), F32),
            pltpu.VMEM(((occ + 1) * tiles * 2, TILE), F32),
            pltpu.VMEM((chunks, 2, cd_width, chunk), BF16),
            pltpu.VMEM((NEAR, part, cd_width), BF16),
            pltpu.VMEM((NEAR, part, cd_width), BF16),
            pltpu.VMEM((far, part, cd_width), F32),
            pltpu.VMEM((far, part, cd_width), F32),
            pltpu.VMEM((groups, 2, per_row, 2, rows // 2, part, cd_width), BF16),
            pltpu.VMEM(shape(0), F32),
            pltpu.VMEM((ab_tiles, TILE), jnp.int32),
        ] + ([pltpu.VMEM((pieces, 2, 2, rows // 2, part, chunk), BF16)] + [pltpu.VMEM(shape(b), BF16) for b in range(1, col_bits)]) * 2 + [
            pltpu.VMEM((pieces, part, chunk), F32),
            pltpu.VMEM((pieces, part, chunk), F32),
            pltpu.SemaphoreType.DMA((1,)),
            pltpu.SemaphoreType.DMA((chunks, 2)),
            pltpu.SemaphoreType.DMA((2, flips)),
            pltpu.SemaphoreType.DMA((2, groups * rows * per_row)),
            pltpu.SemaphoreType.DMA((2, col_bits, pieces)),
            pltpu.SemaphoreType.DMA((2, pieces)),
            pltpu.SemaphoreType.DMA((groups,)),
        ] + ([
            pltpu.SemaphoreType.DMA((2, col_bits, spare)),
            pltpu.VMEM((spare, 2) + (2,) * col_bits + (part, chunk), F32),
        ] + [pltpu.VMEM((spare, 2) + (2,) * (col_bits - 1 - b) + (part, chunk), BF16) for b in range(col_bits)] * 2 if spare else []),
        compiler_params=pltpu.CompilerParams(
            collective_id=0, has_side_effects=True, vmem_limit_bytes=60 * 1024 * 1024),
    )(pairs, mirror.reshape(-1, TILE), screen, integrals)
    divisors = denominators.reshape(own, 2, ab_tiles, TILE).transpose(0, 2, 1, 3).reshape(own * ab_tiles * 2, TILE)
    update = out / divisors
    return update.reshape(own, ab_tiles, 2, TILE).transpose(0, 2, 1, 3).reshape(own, 2, ab_width)


def solution(mesh):
    in_specs = (
        P("row", None, "col"),
        P(None, "col", "row"),
        P(None, "col", "row"),
        P(),
        P("col", None, "row"),
    )
    out_specs = P("col", None, "row")
    return jax.shard_map(body, mesh=mesh, in_specs=in_specs, out_specs=out_specs, check_vma=False)
```
